128 devices in a mesh: wide: 32 (over z, x, core), narrow: 4 (over y).
Axes of the slice: x: 4, y: 4, z: 4, core: 2. Of those that a mesh axis runs over, the one named last changes fastest.
Arguments:
- amps: bfloat16 [256, 128, 128], P(('wide', 'narrow')), may hold values from -4 to 4
- resp: bfloat16 [256, 128, 128], P(('wide', 'narrow')), may hold values from -4 to 4
- trans: bfloat16 [256, 512, 128], P(('wide', 'narrow')), may hold values from -0.375 to 0.375
- ints: bfloat16 [256, 128, 128], P(('wide', 'narrow')), may hold values from -6 to 6
- energies: float32 [256, 128], P(('wide', 'narrow')), may hold values from 0.5 to 4
- couple: float32 [256, 48], P(('wide', 'narrow')), may hold values from -1 to 1
- readers: int32 [256, 48], P(('wide', 'narrow')), may hold values from 0 to 63, as said below
- domains: int32 [256, 4], replicated, may hold values from 0 to 7, as said below
- integrals: bfloat16 [1024, 512], P(None, 'narrow'), may hold values from -0.01171875 to 0.01171875
Outputs:
- new_amps: float32 [256, 128, 128], P(('wide', 'narrow'))
- new_resp: float32 [256, 128, 128], P(('wide', 'narrow'))
- response: float32 [1024, 512], P('wide', 'narrow')
The draws below stay inside these ranges and needn't reach their ends.
Inputs may be any that keep to these rules, and one draw needn't show every extreme that they name: `readers`: each row lists 48 different positions among the 64 pairs of the same narrow index. `domains`: each row lists 4 different function blocks.
All inputs are finite; a program needn't handle non-finite values.
Results may differ from the reference program's by a relative error of at most 0.015.
Values may be sent and summed in bfloat16 or wider, within the bound.
A program may use at most 64 MiB of HBM per device.

```python
import math
import jax
import jax.numpy as jnp
from jax import lax

NPNO = 128
NFUN = 512
BLK = 128
NFB = 8
NCOL = 512
PAIRS_DEV = 2
DOM_BLK = 4
NBAS = 1024
ROW_PAIRS = 64
READERS = 48
PAIRS = 256
N_WIDE = 32
N_NARROW = 4


def draw_readers(key, part):
    scores = jax.random.randint(key, (PAIRS, ROW_PAIRS), 0, 1 << 20) * ROW_PAIRS + jnp.arange(ROW_PAIRS, dtype=jnp.int32)[None, :]
    order = jnp.argsort(scores, axis=1, stable=True)
    return order[:, :READERS].astype(jnp.int32)


def draw_domains(key, part):
    scores = jax.random.randint(key, (PAIRS, NFB), 0, 1 << 20) * NFB + jnp.arange(NFB, dtype=jnp.int32)[None, :]
    order = jnp.argsort(scores, axis=1, stable=True)
    return order[:, :DOM_BLK].astype(jnp.int32)


def level_of(key, shape, cuts, low, top_value):
    level = 1.0
    for dim, parts in cuts:
        draws = jax.random.uniform(jax.random.fold_in(jax.random.fold_in(key, 6), dim), (parts,), jnp.float32, low / len(cuts), top_value / len(cuts))
        level = level * jnp.repeat(jnp.exp(draws), shape[dim] // parts).reshape((-1,) + (1,) * (len(shape) - 1 - dim))
    return level


def scatter_about(key, extent, scale, most, split=(), kind=jnp.bfloat16):
    entries = jax.random.normal(key, extent, jnp.float32) * scale
    if len(split) > 0:
        entries = level_of(key, extent, split, -0.22, 0.18) * entries
    return jnp.clip(entries, min=-most, max=most).astype(kind)


def setup_inputs(seed: int = 0) -> dict:
    keys = jax.random.split(jax.random.key(seed), 10)
    amps = scatter_about(keys[0], (PAIRS, NPNO, NPNO), 0.5, 4.0, ((0, 128),))
    resp = scatter_about(keys[1], (PAIRS, NPNO, NPNO), 0.5, 4.0, ((0, 128),))
    trans = scatter_about(keys[2], (PAIRS, NFUN, NPNO), (NFUN // 2) ** -0.5, 0.375, ((0, 128),))
    ints = scatter_about(keys[3], (PAIRS, NPNO, NPNO), 1.0, 6.0, ((0, 128),))
    energies = jnp.clip(jnp.exp(math.log(4.0) - 2.0794415 * jax.random.uniform(keys[4], (PAIRS, NPNO), jnp.float32) ** level_of(keys[4], (PAIRS, NPNO), ((0, 128),), -0.2, 0.2)), 0.5, 4.0)
    couple = scatter_about(keys[5], (PAIRS, READERS), 0.2, 1.0, ((0, 128),), jnp.float32)
    readers = draw_readers(jax.random.fold_in(keys[9], 71), 0)
    domains = draw_domains(jax.random.fold_in(keys[9], 71), 0)
    integrals = scatter_about(keys[8], (NBAS, NCOL), (256 * NBAS) ** -0.5, 0.01171875, ((1, 4),))
    return dict(amps=amps, resp=resp, trans=trans, ints=ints, energies=energies, couple=couple, readers=readers, domains=domains, integrals=integrals)


def to_rows(values):
    rest = values.shape[1:]
    grouped = values.reshape((N_WIDE, N_NARROW, PAIRS_DEV) + rest)
    return jnp.swapaxes(grouped, 0, 1).reshape((N_NARROW, N_WIDE * PAIRS_DEV) + rest)


def reader_terms(own_q, own_dom, their_q, their_dom, their_amps):
    blocks = own_q.shape[0]
    reader_count = their_q.shape[0]
    matches = (own_dom[None, :, None] == their_dom[:, None, :]).astype(jnp.float32)
    split_q = their_q.reshape(reader_count, blocks, BLK, NPNO).astype(jnp.float32)
    shifted = jnp.einsum('sab,sbfp->safp', matches, split_q).astype(jnp.bfloat16)
    intersection = jnp.einsum('afp,safq->spq', own_q.astype(jnp.float32), shifted.astype(jnp.float32)).astype(jnp.bfloat16)
    halfway = jnp.einsum('spq,sqc->spc', intersection.astype(jnp.float32), their_amps.astype(jnp.float32)).astype(jnp.bfloat16)
    halfway = halfway.reshape(reader_count, NPNO, 2, NPNO)
    return jnp.einsum('spkc,sqc->skpq', halfway.astype(jnp.float32), intersection.astype(jnp.float32))


def reference(amps, resp, trans, ints, energies, couple, readers, domains, integrals):
    dom_blk = NFUN // BLK
    pair_amps = jnp.concatenate([amps, resp], axis=2)
    q_rows = to_rows(trans)
    amp_rows = to_rows(pair_amps)
    dom_rows = to_rows(domains)

    def one_pair(position):
        row_index = (position // PAIRS_DEV) % N_NARROW
        picks = readers[position]
        contrib = reader_terms(trans[position].reshape(dom_blk, BLK, NPNO), domains[position],
                               q_rows[row_index, picks], dom_rows[row_index, picks], amp_rows[row_index, picks])
        return jnp.einsum('s,skpq->kpq', couple[position], contrib)

    coupled = lax.map(one_pair, jnp.arange(PAIRS, dtype=jnp.int32))
    amps_f = amps.astype(jnp.float32)
    resp_f = resp.astype(jnp.float32)
    denominator = energies[:, :, None] + energies[:, None, :]
    new_amps = amps_f - 0.5 * (ints.astype(jnp.float32) + denominator * amps_f + coupled[:, 0]) / denominator
    new_resp = resp_f - 0.5 * (amps_f + denominator * resp_f + coupled[:, 1]) / denominator
    amps_b = new_amps.astype(jnp.bfloat16).astype(jnp.float32)
    resp_b = new_resp.astype(jnp.bfloat16).astype(jnp.float32)
    weights = 0.5 * (jnp.einsum('gpc,gqc->gpq', amps_b, resp_b) + jnp.einsum('gpc,gqc->gpq', resp_b, amps_b))
    weights = weights.astype(jnp.bfloat16)
    block_ids = jnp.arange(NFB, dtype=jnp.int32)

    def density_step(total, items):
        q_one, dom_one, w_one = items
        place = (block_ids[:, None] == dom_one[None, :]).astype(jnp.float32)
        full_q = jnp.einsum('nd,dfp->nfp', place, q_one.reshape(dom_blk, BLK, NPNO).astype(jnp.float32))
        full_q = full_q.reshape(NBAS, NPNO).astype(jnp.bfloat16)
        left = jnp.dot(full_q, w_one, preferred_element_type=jnp.float32).astype(jnp.bfloat16)
        return total + jnp.dot(left, full_q.T, preferred_element_type=jnp.float32), None

    density, _ = lax.scan(density_step, jnp.zeros((NBAS, NBAS), jnp.float32), (trans, domains, weights))
    response = jnp.dot(density, integrals.astype(jnp.float32), precision=lax.Precision.HIGHEST)
    return new_amps, new_resp, response
```

```python
import jax
import jax.numpy as jnp
from jax import lax
from jax.experimental import pallas as pl
from jax.experimental.pallas import tpu as pltpu
from jax.sharding import PartitionSpec as P

MESH = pl.DeviceIdType.MESH
F32 = jnp.float32
BF16 = jnp.bfloat16
RING = 4
PIECES = 32
ROWS = 256

QH, TH, ZH, QG, CG, RG, XA, RS, WB, PC = 0, 16, 32, 48, 56, 60, 64, 68, 74, 82
N_RECV = PC + PIECES
N_SEND = 112
PIECE_SEND = 80


def dot(a, b):
    return jnp.dot(a, b, preferred_element_type=F32)


def dot_nt(a, b):
    return lax.dot_general(a, b, (((1,), (1,)), ((), ())), preferred_element_type=F32)


def dot_tn(a, b):
    return lax.dot_general(a, b, (((0,), (0,)), ((), ())), preferred_element_type=F32)


def kernel(
    amps, resp, trans, ints, energies, couple, readers, domains, integrals,
    out_t, out_z, out_r,
    qh, th, zh, qg, at, sall, hall, xall, yall, fsel, lall, wb, coef, cg, rg,
    rs_send, rs_recv, obuf, rbuf, local_sem, send_sem, recv_sem,
):
    wide = lax.axis_index("wide")
    y = lax.axis_index("narrow")
    c = lax.rem(wide, 2)
    x = lax.rem(wide // 2, RING)
    z = wide // (2 * RING)

    def device(dz=0, dx=0, dc=0, dy=0):
        zz, xx = lax.rem(z + dz, RING), lax.rem(x + dx, RING)
        return ((zz * RING + xx) * 2 + lax.rem(c + dc, 2), lax.rem(y + dy, RING))

    sends = []

    def send(src, dst, recv, where):
        copy = pltpu.make_async_remote_copy(
            src_ref=src, dst_ref=dst, send_sem=send_sem.at[len(sends)],
            recv_sem=recv_sem.at[recv], device_id=where, device_id_type=MESH,
        )
        sends.append(copy)
        copy.start()

    def arrive(ref, recv):
        pltpu.make_async_remote_copy(
            src_ref=ref, dst_ref=ref, send_sem=send_sem.at[0],
            recv_sem=recv_sem.at[recv], device_id=device(dc=1), device_id_type=MESH,
        ).wait_recv()

    up_z, down_z = device(dz=1), device(dz=3)
    up_x, down_x = device(dx=1), device(dx=3)
    sibling = device(dc=1)

    locals_ = []
    for p in range(2):
        for src, dst in (
            (trans.at[p], qh.at[p]), (amps.at[p], th.at[p]), (resp.at[p], zh.at[p]),
            (trans.at[p], qg.at[p]),
        ):
            locals_.append((src, dst))
    locals_.append((couple, cg.at[0]))
    locals_.append((readers, rg.at[0]))
    locals_.append((integrals, xall.at[0]))
    copies = [
        pltpu.make_async_copy(src, dst, local_sem.at[i]) for i, (src, dst) in enumerate(locals_)
    ]
    for copy in copies:
        copy.start()

    barrier = pltpu.get_barrier_semaphore()

    @pl.loop(1, PIECES)
    def _(i):
        where = device(dx=lax.rem(i // 2, RING), dc=lax.rem(i, 2), dy=i // 8)
        pl.semaphore_signal(barrier, inc=1, device_id=where, device_id_type=MESH)

    for where in (up_z, down_z):
        pl.semaphore_signal(barrier, inc=1, device_id=where, device_id_type=MESH)
    for copy in copies:
        copy.wait()
    pl.semaphore_wait(barrier, PIECES + 1)

    def send_pair(s, to, where):
        send(qh.at[s], qh.at[to], QH + to, where)
        send(th.at[s], th.at[to], TH + to, where)
        send(zh.at[s], zh.at[to], ZH + to, where)

    def arrive_pair(s):
        arrive(qh.at[s], QH + s)
        arrive(th.at[s], TH + s)
        arrive(zh.at[s], ZH + s)

    def send_g(s, to, where):
        send(qg.at[s], qg.at[to], QG + to, where)

    def arrive_g(s):
        arrive(qg.at[s], QG + s)

    send_pair(0, 4, up_z)
    send_pair(1, 5, down_z)
    send_g(0, 6, up_x)
    send_g(1, 3, down_x)
    send_pair(0, 2, sibling)
    send_pair(1, 3, sibling)
    send_pair(1, 8, up_z)
    send_pair(0, 9, down_z)
    send_g(1, 7, up_x)
    send_g(0, 2, down_x)
    for d in range(1, RING):
        send(cg.at[0], cg.at[RING - d], CG + RING - d, device(dx=d))
        send(rg.at[0], rg.at[RING - d], RG + RING - d, device(dx=d))
    for d in (1, 3, 2):
        send(xall.at[0], xall.at[RING - d], XA + RING - d, device(dy=d))

    def domain_of(index):
        return [domains[index, a] for a in range(4)]

    def build_at(k):
        index = (
            ((z * RING + lax.rem(x + k // 2, RING)) * 2 + c) * RING + y
        ) * 2 + lax.rem(k, 2)
        own = domain_of(index)
        turned = [jnp.transpose(qg[k, a * 128:(a + 1) * 128, :]) for a in range(4)]
        zero = jnp.zeros((128, 128), BF16)
        rows = pl.ds(pl.multiple_of(k * 128, 128), 128)
        for block in range(8):
            value = zero
            for a in range(4):
                value = lax.select(own[a] == block, turned[a], value)
            at[block, rows, :] = value

    def each(low, high, body):
        def step(i, carry):
            body(i)
            return carry
        lax.fori_loop(low, high, step, 0)

    def place(s):
        group, inner = s // 4, lax.rem(s, 4)
        flip, i = inner // 2, lax.rem(inner, 2)
        near = jnp.where(i == 0, 3, 1)
        dz = jnp.where(group == 0, 0, jnp.where(group == 3, 2, near))
        pair = jnp.where(group == 2, 1 - i, i)
        return lax.rem(z + dz, RING), lax.rem(c + flip, 2), pair

    def index_of(s):
        zz, cc, pair = place(s)
        return (((zz * RING + x) * 2 + cc) * RING + y) * 2 + pair

    each(0, 2, build_at)
    arrive_g(6)
    send_g(6, 4, up_x)
    arrive_g(3)
    send_g(3, 5, down_x)
    each(3, 4, build_at)
    each(6, 7, build_at)
    for slot in (4, 5):
        arrive_pair(slot)
        send_pair(slot, 12 if slot == 4 else 13, up_z if slot == 4 else down_z)
        send_pair(slot, slot + 2, sibling)
    arrive_g(2)
    each(2, 3, build_at)
    arrive_g(7)
    each(7, 8, build_at)

    for d in range(1, RING):
        arrive(cg.at[d], CG + d)
        arrive(rg.at[d], RG + d)
    slots = lax.broadcasted_iota(jnp.int32, (16, 48), 0)
    zz, cc, pair = place(slots)
    position = ((zz * RING + x) * 2 + cc) * 2 + pair
    for k in range(8):
        row = rg[k // 2, k % 2:k % 2 + 1, :]
        weight = cg[k // 2, k % 2:k % 2 + 1, :]
        picked = jnp.where(position == row, weight, 0.0)
        coef[k] = jnp.broadcast_to(jnp.sum(picked, axis=1, keepdims=True), (16, 128))

    arrive_g(4)
    each(4, 5, build_at)
    arrive_g(5)
    each(5, 6, build_at)

    def tile(s):
        theirs = domain_of(index_of(s))
        columns = pl.ds(pl.multiple_of(s * 128, 128), 128)
        both = jnp.concatenate([th[s], zh[s]], axis=1)
        for low in range(0, 1024, ROWS):
            left = jnp.concatenate(
                [at[theirs[b], low:low + ROWS, :] for b in range(4)], axis=1
            )
            inter = dot(left, qh[s]).astype(BF16)
            half = dot(inter, both)
            for i in range(ROWS // 128):
                k = low // 128 + i
                rows = slice(i * 128, (i + 1) * 128)
                weight = coef[k, pl.ds(s, 1), :]
                sall[k, :, columns] = inter[rows]
                hall[k, 0:128, columns] = (half[rows, 0:128] * weight).astype(BF16)
                hall[k, 128:256, columns] = (half[rows, 128:256] * weight).astype(BF16)

    for slot in (2, 3):
        arrive_pair(slot)
    each(0, 4, tile)
    for slot in (6, 7):
        arrive_pair(slot)
    each(4, 8, tile)
    for slot in (8, 9):
        arrive_pair(slot)
        send_pair(slot, slot + 2, sibling)
    for slot in (12, 13):
        arrive_pair(slot)
        send_pair(slot, slot + 2, sibling)
    for slot in (10, 11):
        arrive_pair(slot)
    each(8, 12, tile)
    for slot in (14, 15):
        arrive_pair(slot)
    each(12, 16, tile)

    def coupled(k):
        return dot_nt(hall[k], sall[k])

    def pass_on(i, value, where):
        rs_send[i] = value.astype(BF16)
        send(rs_send.at[i], rs_recv.at[i], RS + i, where)

    pass_on(0, coupled(4), up_x)
    pass_on(1, coupled(5), down_x)
    pass_on(2, coupled(3), up_x)
    pass_on(3, coupled(6), down_x)
    part0, part1 = coupled(2), coupled(7)
    arrive(rs_recv.at[0], RS + 0)
    pass_on(4, part0 + rs_recv[0].astype(F32), up_x)
    arrive(rs_recv.at[1], RS + 1)
    pass_on(5, part1 + rs_recv[1].astype(F32), down_x)
    for d in range(1, RING):
        arrive(xall.at[d], XA + d)

    def own_slot(j):
        return (j // 2) * 4 + lax.rem(j, 2)

    def columns_of(j):
        s = own_slot(j)
        theirs = domain_of(index_of(s))
        wide_rows = [
            jnp.concatenate([xall[d, theirs[b]] for d in range(RING)], axis=1) for b in range(4)
        ]
        rows = pl.ds(pl.multiple_of(j * 128, 128), 128)
        yall[rows, :] = dot_tn(qh[s], jnp.concatenate(wide_rows, axis=0)).astype(BF16)
        zero = jnp.zeros((128, 128), BF16)
        for i in range(2):
            value = zero
            for b in range(4):
                value = lax.select(
                    theirs[b] == 2 * z + i, qh[s, b * 128:(b + 1) * 128, :], value
                )
            fsel[j, i * 128:(i + 1) * 128, :] = value

    each(0, 8, columns_of)

    own = [coupled(0), coupled(1)]
    for p in range(2):
        near, far = ((3, 4), (2, 5))[p]
        arrive(rs_recv.at[near], RS + near)
        arrive(rs_recv.at[far], RS + far)
        total = own[p] + rs_recv[near].astype(F32) + rs_recv[far].astype(F32)
        across = jnp.broadcast_to(energies[p:p + 1, :], (128, 128))
        denom = across + jnp.transpose(across)
        amp = th[p].astype(F32)
        res = zh[p].astype(F32)
        new_t = amp - 0.5 * (ints[p].astype(F32) + denom * amp + total[0:128]) / denom
        new_z = res - 0.5 * (amp + denom * res + total[128:256]) / denom
        out_t[p] = new_t
        out_z[p] = new_z
        product = dot_nt(new_t.astype(BF16), new_z.astype(BF16))
        wb[p] = (0.5 * (product + jnp.transpose(product))).astype(BF16)

    def send_w(s, to, where):
        send(wb.at[s], wb.at[to], WB + to, where)

    send_w(0, 2, up_z)
    send_w(1, 3, down_z)
    send_w(1, 4, up_z)
    send_w(0, 5, down_z)
    arrive(wb.at[2], WB + 2)
    send_w(2, 6, up_z)
    arrive(wb.at[3], WB + 3)
    send_w(3, 7, down_z)

    def left_of(j):
        columns = pl.ds(pl.multiple_of(j * 128, 128), 128)
        lall[:, columns] = dot(fsel[j], wb[j]).astype(BF16)

    each(0, 4, left_of)
    for j in (4, 5):
        arrive(wb.at[j], WB + j)
    each(4, 6, left_of)
    for j in (6, 7):
        arrive(wb.at[j], WB + j)
    each(6, 8, left_of)
    partial = dot(lall[...], yall[...])
    for d in range(RING):
        for i in range(8):
            obuf[d, i] = partial[i * 32:(i + 1) * 32, d * 128:(d + 1) * 128].astype(BF16)

    def piece(i):
        dx, dc, dy = lax.rem(i // 2, RING), lax.rem(i, 2), i // 8
        return pltpu.make_async_remote_copy(
            src_ref=obuf.at[dy, lax.rem(x + dx, RING) * 2 + lax.rem(c + dc, 2)],
            dst_ref=rbuf.at[i], send_sem=send_sem.at[PIECE_SEND + i],
            recv_sem=recv_sem.at[PC + i], device_id=device(dx=dx, dc=dc, dy=dy),
            device_id_type=MESH,
        )

    each(1, PIECES, lambda i: piece(i).start())
    for copy in sends:
        copy.wait_send()
    out_r[...] = obuf[0, x * 2 + c].astype(F32)

    def take(i):
        piece(i).wait_recv()
        out_r[...] += rbuf[i].astype(F32)

    each(1, PIECES, take)
    each(1, PIECES, lambda i: piece(i).wait_send())


def per_device(amps, resp, trans, ints, energies, couple, readers, domains, integrals):
    vmem = pl.BlockSpec(memory_space=pltpu.VMEM)
    anywhere = pl.BlockSpec(memory_space=pl.ANY)
    dma = pltpu.SemaphoreType.DMA
    return pl.pallas_call(
        kernel,
        out_shape=(
            jax.ShapeDtypeStruct((2, 128, 128), F32),
            jax.ShapeDtypeStruct((2, 128, 128), F32),
            jax.ShapeDtypeStruct((32, 128), F32),
        ),
        in_specs=[
            anywhere, anywhere, anywhere, vmem, vmem, vmem, vmem,
            pl.BlockSpec(memory_space=pltpu.SMEM), anywhere,
        ],
        out_specs=(vmem, vmem, vmem),
        scratch_shapes=[
            pltpu.VMEM((16, 512, 128), BF16),
            pltpu.VMEM((16, 128, 128), BF16),
            pltpu.VMEM((16, 128, 128), BF16),
            pltpu.VMEM((8, 512, 128), BF16),
            pltpu.VMEM((8, 1024, 128), BF16),
            pltpu.VMEM((8, 128, 2048), BF16),
            pltpu.VMEM((8, 256, 2048), BF16),
            pltpu.VMEM((4, 8, 128, 128), BF16),
            pltpu.VMEM((1024, 512), BF16),
            pltpu.VMEM((8, 256, 128), BF16),
            pltpu.VMEM((256, 1024), BF16),
            pltpu.VMEM((8, 128, 128), BF16),
            pltpu.VMEM((8, 16, 128), F32),
            pltpu.VMEM((4, 2, 48), F32),
            pltpu.VMEM((4, 2, 48), jnp.int32),
            pltpu.VMEM((6, 256, 128), BF16),
            pltpu.VMEM((6, 256, 128), BF16),
            pltpu.VMEM((4, 8, 32, 128), BF16),
            pltpu.VMEM((PIECES, 32, 128), BF16),
            dma((16,)), dma((N_SEND,)), dma((N_RECV,)),
        ],
        compiler_params=pltpu.CompilerParams(
            collective_id=0, has_side_effects=True, vmem_limit_bytes=60 * 1024 * 1024
        ),
    )(amps, resp, trans, ints, energies, couple, readers, domains, integrals.reshape(8, 128, 128))


def solution(mesh):
    pairs3 = P(("wide", "narrow"), None, None)
    pairs2 = P(("wide", "narrow"), None)
    return jax.shard_map(
        per_device,
        mesh=mesh,
        in_specs=(
            pairs3, pairs3, pairs3, pairs3, pairs2, pairs2, pairs2, P(), P(None, "narrow"),
        ),
        out_specs=(pairs3, pairs3, P("wide", "narrow")),
        check_vma=False,
    )
```

```python
import jax
import jax.numpy as jnp
from jax import lax
from jax.experimental import pallas as pl
from jax.experimental.pallas import tpu as pltpu
from jax.sharding import PartitionSpec as P

MESH = pl.DeviceIdType.MESH
F32 = jnp.float32
BF16 = jnp.bfloat16
RING = 4
PIECES = 32
HALF = 512
G_PLACE = ((0, 0), (0, 1), (3, 0), (1, 1), (3, 1), (1, 0), (2, 0), (2, 1))

HB, QG, CG, RG, XA, RS, WB, PC = 0, 16, 24, 28, 32, 40, 46, 54
N_RECV = PC + PIECES
N_SEND = 112
PIECE_SEND = 80


def dot(a, b):
    return jnp.dot(a, b, preferred_element_type=F32)


def dot_nt(a, b):
    return lax.dot_general(a, b, (((1,), (1,)), ((), ())), preferred_element_type=F32)


def dot_tn(a, b):
    return lax.dot_general(a, b, (((0,), (0,)), ((), ())), preferred_element_type=F32)


def each(low, high, body):
    def step(i, carry):
        body(i)
        return carry
    lax.fori_loop(low, high, step, 0)


def kernel(
    amps, resp, trans, ints, energies, couple, readers, domains, integrals,
    out_t, out_z, out_r,
    hb, qg, at, sall, hall, xall, yall, fsel, lall, wb, coef, cg, rg, dom, ex, en,
    base, scale, new, rs_send, rs_recv, obuf, rbuf, rsum,
    local_sem, send_sem, recv_sem, known,
):
    wide = lax.axis_index("wide")
    y = lax.axis_index("narrow")
    c = lax.rem(wide, 2)
    x = lax.rem(wide // 2, RING)
    z = wide // (2 * RING)

    def device(dz=0, dx=0, dc=0, dy=0):
        zz, xx = lax.rem(z + dz, RING), lax.rem(x + dx, RING)
        return ((zz * RING + xx) * 2 + lax.rem(c + dc, 2), lax.rem(y + dy, RING))

    up_z, down_z = device(dz=1), device(dz=3)
    up_x, down_x = device(dx=1), device(dx=3)
    up_y, down_y = device(dy=1), device(dy=3)
    sibling = device(dc=1)

    def tell(sem, *where):
        for one in where:
            pl.semaphore_signal(sem, inc=1, device_id=one, device_id_type=MESH)

    barrier = pltpu.get_barrier_semaphore()
    tell(barrier, up_z, down_z, up_x, down_x, sibling, up_y, down_y)

    moves = []
    for p in range(2):
        moves += [
            (trans.at[p], hb.at[p, 0:512]), (amps.at[p], hb.at[p, 512:640]),
            (resp.at[p], hb.at[p, 640:768]),
        ]
    moves += [
        (couple, cg.at[0]), (readers, rg.at[0]), (integrals, xall.at[0]), (domains, dom),
        (ints, ex), (energies, en),
    ]
    copies = [
        pltpu.make_async_copy(src, dst, local_sem.at[i]) for i, (src, dst) in enumerate(moves)
    ]
    for copy in copies:
        copy.start()
    for copy in copies:
        copy.wait()
    pl.semaphore_wait(barrier, 7)

    sends = []

    def send(src, dst, recv, where):
        copy = pltpu.make_async_remote_copy(
            src_ref=src, dst_ref=dst, send_sem=send_sem.at[len(sends)],
            recv_sem=recv_sem.at[recv], device_id=where, device_id_type=MESH,
        )
        sends.append(copy)
        copy.start()

    def arrive(ref, recv):
        pltpu.make_async_remote_copy(
            src_ref=ref, dst_ref=ref, send_sem=send_sem.at[0],
            recv_sem=recv_sem.at[recv], device_id=sibling, device_id_type=MESH,
        ).wait_recv()

    def send_pair(s, to, where):
        send(hb.at[s], hb.at[to], HB + to, where)

    def arrive_pair(*slots):
        for s in slots:
            arrive(hb.at[s], HB + s)

    def send_g(src, to, where):
        send(src, qg.at[to], QG + to, where)

    def arrive_g(*slots):
        for s in slots:
            arrive(qg.at[s], QG + s)

    def send_x(d, half, to, where):
        rows = slice(half * 4, half * 4 + 4)
        send(xall.at[d, rows], xall.at[to, rows], XA + to * 2 + half, where)

    def arrive_x(d, half):
        arrive(xall.at[d, half * 4:half * 4 + 4], XA + d * 2 + half)

    send_pair(0, 4, up_z)
    send_pair(1, 5, down_z)
    send_g(hb.at[0, 0:512], 2, up_x)
    send_g(hb.at[1, 0:512], 3, down_x)
    send_pair(0, 2, sibling)
    send_pair(1, 3, sibling)
    send_pair(1, 8, up_z)
    send_pair(0, 9, down_z)
    send_g(hb.at[1, 0:512], 4, up_x)
    send_g(hb.at[0, 0:512], 5, down_x)
    for src, base_sem in ((cg, CG), (rg, RG)):
        send(src.at[0], src.at[3], base_sem + 3, up_x)
        send(src.at[0], src.at[1], base_sem + 1, down_x)
    send_x(0, 0, 3, up_y)
    send_x(0, 1, 1, down_y)
    send_x(0, 1, 3, up_y)
    send_x(0, 0, 1, down_y)

    def domain_of(index):
        return [dom[a, index] for a in range(4)]

    zero = jnp.zeros((128, 128), BF16)

    def pair_of_g(k):
        return G_PLACE[k]

    def build_at(k):
        dx, pair = pair_of_g(k)
        own = domain_of((((z * RING + lax.rem(x + dx, RING)) * 2 + c) * RING + y) * 2 + pair)
        source = hb if k < 2 else qg
        turned = [jnp.transpose(source[k, a * 128:(a + 1) * 128, :]) for a in range(4)]
        for block in range(8):
            value = zero
            for a in range(4):
                value = lax.select(own[a] == block, turned[a], value)
            at[block, k * 128:(k + 1) * 128, :] = value

    def place(s):
        group, inner = s // 4, lax.rem(s, 4)
        flip, i = inner // 2, lax.rem(inner, 2)
        near = jnp.where(i == 0, 3, 1)
        dz = jnp.where(group == 0, 0, jnp.where(group == 3, 2, near))
        pair = jnp.where(group == 2, 1 - i, i)
        return lax.rem(z + dz, RING), lax.rem(c + flip, 2), pair

    def index_of(s):
        zz, cc, pair = place(s)
        return (((zz * RING + x) * 2 + cc) * RING + y) * 2 + pair

    def tile(i, low):
        pair = (2 * i, 2 * i + 1)
        inters = []
        for s in pair:
            theirs = domain_of(index_of(s))
            left = jnp.concatenate([at[theirs[b], low:low + HALF, :] for b in range(4)], axis=1)
            inters.append(dot(left, hb[s, 0:512, :]).astype(BF16))
        for s, inter in zip(pair, inters):
            columns = pl.ds(pl.multiple_of(s * 128, 128), 128)
            both = jnp.concatenate([hb[s, 512:640, :], hb[s, 640:768, :]], axis=1)
            half = dot(inter, both)
            for j in range(HALF // 128):
                k = low // 128 + j
                rows = slice(j * 128, (j + 1) * 128)
                weight = coef[k, pl.ds(s, 1), :]
                sall[k, :, columns] = inter[rows]
                hall[k, 0:128, columns] = (half[rows, 0:128] * weight).astype(BF16)
                hall[k, 128:256, columns] = (half[rows, 128:256] * weight).astype(BF16)

    def coefficients(ks):
        slots = lax.broadcasted_iota(jnp.int32, (16, 48), 0)
        zz, cc, pair = place(slots)
        position = ((zz * RING + x) * 2 + cc) * 2 + pair
        for k in ks:
            dx, p = pair_of_g(k)
            row = rg[dx, p:p + 1, :]
            weight = cg[dx, p:p + 1, :]
            picked = jnp.where(position == row, weight, 0.0)
            coef[k] = jnp.broadcast_to(jnp.sum(picked, axis=1, keepdims=True), (16, 128))

    build_at(0)
    build_at(1)
    for p in range(2):
        across = jnp.broadcast_to(en[p:p + 1, :], (128, 128))
        denom = across + jnp.transpose(across)
        amp = hb[p, 512:640, :].astype(F32)
        res = hb[p, 640:768, :].astype(F32)
        scale[p] = 0.5 / denom
        base[p, 0] = amp - 0.5 * (ex[p].astype(F32) + denom * amp) / denom
        base[p, 1] = res - 0.5 * (amp + denom * res) / denom
    for src, base_sem in ((cg, CG), (rg, RG)):
        arrive(src.at[3], base_sem + 3)
        send(src.at[3], src.at[2], base_sem + 2, up_x)
        arrive(src.at[1], base_sem + 1)
    tell(known.at[0], up_x, down_x)
    coefficients((0, 1, 2, 3, 4, 5))
    arrive_g(2)
    send_g(qg.at[2], 6, up_x)
    arrive_g(3)
    send_g(qg.at[3], 7, down_x)
    build_at(2)
    build_at(3)
    arrive_pair(2, 3)
    each(0, 2, lambda i: tile(i, 0))
    arrive_x(3, 0)
    send_x(3, 0, 2, up_y)
    arrive_x(1, 1)
    send_x(1, 1, 2, down_y)
    arrive_pair(4)
    send_pair(4, 12, up_z)
    send_pair(4, 6, sibling)
    arrive_pair(5)
    send_pair(5, 13, down_z)
    send_pair(5, 7, sibling)
    for src, base_sem in ((cg, CG), (rg, RG)):
        arrive(src.at[2], base_sem + 2)
    coefficients((6, 7))
    arrive_g(4, 5)
    build_at(4)
    build_at(5)
    arrive_pair(6, 7)
    each(2, 4, lambda i: tile(i, 0))
    pl.semaphore_wait(known.at[0], 2)
    tell(known.at[1], sibling)
    arrive_g(6, 7)
    build_at(6)
    build_at(7)
    arrive_pair(8)
    send_pair(8, 10, sibling)
    arrive_pair(9)
    send_pair(9, 11, sibling)
    each(0, 4, lambda i: tile(i, HALF))
    arrive_pair(10, 11)

    def whole(i):
        tile(i, 0)
        tile(i, HALF)

    each(4, 6, whole)
    pl.semaphore_wait(known.at[1], 1)
    tell(known.at[2], up_y, down_y)
    arrive_pair(12)
    send_pair(12, 14, sibling)
    arrive_pair(13)
    send_pair(13, 15, sibling)
    each(6, 7, whole)
    arrive_pair(14, 15)
    each(7, 8, whole)

    def coupled(k):
        return dot_nt(hall[k], sall[k])

    def pass_on(i, value, where):
        rs_send[i] = value.astype(BF16)
        send(rs_send.at[i], rs_recv.at[i], RS + i, where)

    pass_on(0, coupled(6), up_x)
    pass_on(1, coupled(7), down_x)
    pass_on(2, coupled(3), up_x)
    pass_on(3, coupled(2), down_x)
    part0, part1 = coupled(5), coupled(4)
    arrive(rs_recv.at[0], RS + 0)
    pass_on(4, part0 + rs_recv[0].astype(F32), up_x)
    arrive(rs_recv.at[1], RS + 1)
    pass_on(5, part1 + rs_recv[1].astype(F32), down_x)
    pl.semaphore_wait(known.at[2], 2)
    tell(known.at[3], up_y, down_y)
    for d, half in ((3, 1), (1, 0), (2, 0), (2, 1)):
        arrive_x(d, half)

    def columns_of(j):
        s = (j // 2) * 4 + lax.rem(j, 2)
        theirs = domain_of(index_of(s))
        wide_rows = [
            jnp.concatenate([xall[d, theirs[b]] for d in range(RING)], axis=1) for b in range(4)
        ]
        rows = pl.ds(pl.multiple_of(j * 128, 128), 128)
        yall[rows, :] = dot_tn(hb[s, 0:512, :], jnp.concatenate(wide_rows, axis=0)).astype(BF16)
        for i in range(2):
            value = zero
            for b in range(4):
                value = lax.select(
                    theirs[b] == 2 * z + i, hb[s, b * 128:(b + 1) * 128, :], value
                )
            fsel[j, i * 128:(i + 1) * 128, :] = value

    each(0, 8, columns_of)
    own = [coupled(0), coupled(1)]
    for p in range(2):
        near, far = ((3, 4), (2, 5))[p]
        arrive(rs_recv.at[near], RS + near)
        arrive(rs_recv.at[far], RS + far)
        total = own[p] + rs_recv[near].astype(F32) + rs_recv[far].astype(F32)
        new_t = base[p, 0] - total[0:128] * scale[p]
        new_z = base[p, 1] - total[128:256] * scale[p]
        new[0, p] = new_t
        new[1, p] = new_z
        product = dot_nt(new_t.astype(BF16), new_z.astype(BF16))
        wb[p] = (0.5 * (product + jnp.transpose(product))).astype(BF16)

    def send_w(s, to, where):
        send(wb.at[s], wb.at[to], WB + to, where)

    send_w(0, 2, up_z)
    send_w(1, 3, down_z)
    send_w(1, 4, up_z)
    send_w(0, 5, down_z)
    outs = [
        pltpu.make_async_copy(new.at[0], out_t, local_sem.at[0]),
        pltpu.make_async_copy(new.at[1], out_z, local_sem.at[1]),
    ]
    for copy in outs:
        copy.start()
    pl.semaphore_wait(known.at[3], 2)

    def left_of(*js):
        for j in js:
            lall[:, j * 128:(j + 1) * 128] = dot(fsel[j], wb[j]).astype(BF16)

    left_of(0, 1)
    arrive(wb.at[2], WB + 2)
    send_w(2, 6, up_z)
    arrive(wb.at[3], WB + 3)
    send_w(3, 7, down_z)
    left_of(2, 3)
    for j in (4, 5):
        arrive(wb.at[j], WB + j)
    left_of(4, 5)
    early = dot(lall[:, 0:768], yall[0:768, :])
    for j in (6, 7):
        arrive(wb.at[j], WB + j)
    left_of(6, 7)

    def piece(i):
        dy, dx, dc = i // 8, (i // 2) % 4, i % 2
        return pltpu.make_async_remote_copy(
            src_ref=obuf.at[dy, lax.rem(x + dx, RING) * 2 + lax.rem(c + dc, 2)],
            dst_ref=rbuf.at[i], send_sem=send_sem.at[PIECE_SEND + i],
            recv_sem=recv_sem.at[PC + i], device_id=device(dx=dx, dc=dc, dy=dy),
            device_id_type=MESH,
        )

    pieces = [None] + [piece(i) for i in range(1, PIECES)]
    for dys in ((2, 3), (0, 1)):
        columns = slice(dys[0] * 128, dys[0] * 128 + 256)
        partial = early[:, columns] + dot(lall[:, 768:1024], yall[768:1024, columns])
        for d in dys:
            for i in range(8):
                block = partial[i * 32:(i + 1) * 32, (d - dys[0]) * 128:(d - dys[0] + 1) * 128]
                obuf[d, i] = block.astype(BF16)
        for d in dys:
            for i in (4, 5, 2, 3, 6, 7, 1, 0):
                if d * 8 + i:
                    pieces[d * 8 + i].start()
    for copy in sends:
        copy.wait_send()
    for copy in outs:
        copy.wait()
    total = obuf[0, x * 2 + c].astype(F32)
    for i in range(1, PIECES):
        pieces[i].wait_recv()
        total = total + rbuf[i].astype(F32)
    rsum[...] = total
    last = pltpu.make_async_copy(rsum, out_r, local_sem.at[2])
    last.start()
    for i in range(1, PIECES):
        pieces[i].wait_send()
    last.wait()


def per_device(amps, resp, trans, ints, energies, couple, readers, domains, integrals):
    anywhere = pl.BlockSpec(memory_space=pl.ANY)
    dma = pltpu.SemaphoreType.DMA
    return pl.pallas_call(
        kernel,
        out_shape=(
            jax.ShapeDtypeStruct((2, 128, 128), F32),
            jax.ShapeDtypeStruct((2, 128, 128), F32),
            jax.ShapeDtypeStruct((32, 128), F32),
        ),
        in_specs=[anywhere] * 9,
        out_specs=(anywhere,) * 3,
        scratch_shapes=[
            pltpu.VMEM((16, 768, 128), BF16),
            pltpu.VMEM((8, 512, 128), BF16),
            pltpu.VMEM((8, 1024, 128), BF16),
            pltpu.VMEM((8, 128, 2048), BF16),
            pltpu.VMEM((8, 256, 2048), BF16),
            pltpu.VMEM((4, 8, 128, 128), BF16),
            pltpu.VMEM((1024, 512), BF16),
            pltpu.VMEM((8, 256, 128), BF16),
            pltpu.VMEM((256, 1024), BF16),
            pltpu.VMEM((8, 128, 128), BF16),
            pltpu.VMEM((8, 16, 128), F32),
            pltpu.VMEM((4, 2, 48), F32),
            pltpu.VMEM((4, 2, 48), jnp.int32),
            pltpu.SMEM((4, 256), jnp.int32),
            pltpu.VMEM((2, 128, 128), BF16),
            pltpu.VMEM((2, 128), F32),
            pltpu.VMEM((2, 2, 128, 128), F32),
            pltpu.VMEM((2, 128, 128), F32),
            pltpu.VMEM((2, 2, 128, 128), F32),
            pltpu.VMEM((6, 256, 128), BF16),
            pltpu.VMEM((6, 256, 128), BF16),
            pltpu.VMEM((4, 8, 32, 128), BF16),
            pltpu.VMEM((PIECES, 32, 128), BF16),
            pltpu.VMEM((32, 128), F32),
            dma((16,)), dma((N_SEND,)), dma((N_RECV,)), pltpu.SemaphoreType.REGULAR((4,)),
        ],
        compiler_params=pltpu.CompilerParams(
            collective_id=0, has_side_effects=True, vmem_limit_bytes=60 * 1024 * 1024
        ),
    )(
        amps, resp, trans, ints, energies, couple, readers, domains.T,
        integrals.reshape(8, 128, 128),
    )


def solution(mesh):
    pairs3 = P(("wide", "narrow"), None, None)
    pairs2 = P(("wide", "narrow"), None)
    return jax.shard_map(
        per_device,
        mesh=mesh,
        in_specs=(
            pairs3, pairs3, pairs3, pairs3, pairs2, pairs2, pairs2, P(), P(None, "narrow"),
        ),
        out_specs=(pairs3, pairs3, P("wide", "narrow")),
        check_vma=False,
    )
```

```python
import jax
import jax.numpy as jnp
from jax import lax
from jax.experimental import pallas as pl
from jax.experimental.pallas import tpu as pltpu
from jax.sharding import PartitionSpec as P

MESH = pl.DeviceIdType.MESH
F32 = jnp.float32
BF16 = jnp.bfloat16
RING = 4
PIECES = 32
HALF = 512
G_PLACE = ((0, 0), (0, 1), (3, 0), (1, 1), (3, 1), (1, 0), (2, 0), (2, 1))

HB, HC, QG, CG, RG, XA, RS, WB, PC = 0, 16, 32, 40, 44, 48, 56, 62, 70
N_RECV = PC + PIECES
N_SEND = 140
PIECE_SEND = 104


def dot(a, b):
    return jnp.dot(a, b, preferred_element_type=F32)


def dot_nt(a, b):
    return lax.dot_general(a, b, (((1,), (1,)), ((), ())), preferred_element_type=F32)


def dot_tn(a, b):
    return lax.dot_general(a, b, (((0,), (0,)), ((), ())), preferred_element_type=F32)


def each(low, high, body):
    def step(i, carry):
        body(i)
        return carry
    lax.fori_loop(low, high, step, 0)


def kernel(
    amps, resp, trans, ints, energies, couple, readers, domains, integrals,
    out_t, out_z, out_r,
    hb, qg, at, sall, hall, xall, yall, fsel, lall, wb, coef, cg, rg, dom, ex, en,
    base, scale, rs_send, rs_recv, obuf, rbuf,
    local_sem, send_sem, recv_sem, known,
):
    wide = lax.axis_index("wide")
    y = lax.axis_index("narrow")
    c = lax.rem(wide, 2)
    x = lax.rem(wide // 2, RING)
    z = wide // (2 * RING)

    def device(dz=0, dx=0, dc=0, dy=0):
        zz, xx = lax.rem(z + dz, RING), lax.rem(x + dx, RING)
        return ((zz * RING + xx) * 2 + lax.rem(c + dc, 2), lax.rem(y + dy, RING))

    up_z, down_z = device(dz=1), device(dz=3)
    up_x, down_x = device(dx=1), device(dx=3)
    up_y, down_y = device(dy=1), device(dy=3)
    sibling = device(dc=1)

    def tell(sem, *where):
        for one in where:
            pl.semaphore_signal(sem, inc=1, device_id=one, device_id_type=MESH)

    barrier = pltpu.get_barrier_semaphore()
    tell(barrier, up_z, down_z, up_x, down_x, sibling, up_y, down_y)

    moves = []
    for p in range(2):
        moves += [
            (trans.at[p], hb.at[p, 0:512]), (amps.at[p], hb.at[p, 512:640]),
            (resp.at[p], hb.at[p, 640:768]),
        ]
    moves += [
        (couple, cg.at[0]), (readers, rg.at[0]), (integrals, xall.at[0]), (domains, dom),
        (ints, ex), (energies, en),
    ]
    copies = [
        pltpu.make_async_copy(src, dst, local_sem.at[i]) for i, (src, dst) in enumerate(moves)
    ]
    for copy in copies:
        copy.start()
    pl.semaphore_wait(barrier, 7)

    sends = []

    def send(src, dst, recv, where):
        copy = pltpu.make_async_remote_copy(
            src_ref=src, dst_ref=dst, send_sem=send_sem.at[len(sends)],
            recv_sem=recv_sem.at[recv], device_id=where, device_id_type=MESH,
        )
        sends.append(copy)
        copy.start()

    def arrive(ref, recv):
        pltpu.make_async_remote_copy(
            src_ref=ref, dst_ref=ref, send_sem=send_sem.at[0],
            recv_sem=recv_sem.at[recv], device_id=sibling, device_id_type=MESH,
        ).wait_recv()

    def send_pair(s, to, where):
        send(hb.at[s], hb.at[to], HB + to, where)

    def arrive_pair(*slots):
        for s in slots:
            arrive(hb.at[s], HB + s)

    PARTS = ((slice(0, 384), HB), (slice(384, 768), HC))

    def send_part(s, part, to, where):
        rows, sem = PARTS[part]
        send(hb.at[s, rows], hb.at[to, rows], sem + to, where)

    def arrive_part(s, part):
        rows, sem = PARTS[part]
        arrive(hb.at[s, rows], sem + s)

    def send_g(src, to, where):
        send(src, qg.at[to], QG + to, where)

    def arrive_g(*slots):
        for s in slots:
            arrive(qg.at[s], QG + s)

    def send_x(d, half, to, where):
        rows = slice(half * 4, half * 4 + 4)
        send(xall.at[d, rows], xall.at[to, rows], XA + to * 2 + half, where)

    def arrive_x(d, half):
        arrive(xall.at[d, half * 4:half * 4 + 4], XA + d * 2 + half)

    def send_own(p, to, where):
        send(trans.at[p], hb.at[to, 0:512], HB + to, where)
        send(amps.at[p], hb.at[to, 512:640], HB + to, where)
        send(resp.at[p], hb.at[to, 640:768], HB + to, where)

    send_own(0, 4, up_z)
    send_own(1, 5, down_z)
    send_g(trans.at[0], 2, up_x)
    send_g(trans.at[1], 3, down_x)
    send_own(0, 2, sibling)
    send_own(1, 3, sibling)
    send_own(1, 8, up_z)
    send_own(0, 9, down_z)
    send_g(trans.at[1], 4, up_x)
    send_g(trans.at[0], 5, down_x)
    for src, dst, base_sem in ((couple, cg, CG), (readers, rg, RG)):
        send(src, dst.at[3], base_sem + 3, up_x)
        send(src, dst.at[1], base_sem + 1, down_x)
    for half, to, where in ((0, 3, up_y), (1, 1, down_y), (1, 3, up_y), (0, 1, down_y)):
        rows = slice(half * 4, half * 4 + 4)
        send(integrals.at[rows], xall.at[to, rows], XA + to * 2 + half, where)
    for copy in copies:
        copy.wait()

    def domain_of(index):
        return [dom[a, index] for a in range(4)]

    zero = jnp.zeros((128, 128), BF16)

    def pair_of_g(k):
        return G_PLACE[k]

    def build_at(k):
        dx, pair = pair_of_g(k)
        own = domain_of((((z * RING + lax.rem(x + dx, RING)) * 2 + c) * RING + y) * 2 + pair)
        source = hb if k < 2 else qg
        turned = [jnp.transpose(source[k, a * 128:(a + 1) * 128, :]) for a in range(4)]
        for block in range(8):
            value = zero
            for a in range(4):
                value = lax.select(own[a] == block, turned[a], value)
            at[block, k * 128:(k + 1) * 128, :] = value

    def place(s):
        group, inner = s // 4, lax.rem(s, 4)
        flip, i = inner // 2, lax.rem(inner, 2)
        near = jnp.where(i == 0, 3, 1)
        dz = jnp.where(group == 0, 0, jnp.where(group == 3, 2, near))
        pair = jnp.where(group == 2, 1 - i, i)
        return lax.rem(z + dz, RING), lax.rem(c + flip, 2), pair

    def index_of(s):
        zz, cc, pair = place(s)
        return (((zz * RING + x) * 2 + cc) * RING + y) * 2 + pair

    def tile(i, low):
        pair = (2 * i, 2 * i + 1)
        inters = []
        for s in pair:
            theirs = domain_of(index_of(s))
            left = jnp.concatenate([at[theirs[b], low:low + HALF, :] for b in range(4)], axis=1)
            inters.append(dot(left, hb[s, 0:512, :]).astype(BF16))
        for s, inter in zip(pair, inters):
            columns = pl.ds(pl.multiple_of(s * 128, 128), 128)
            both = jnp.concatenate([hb[s, 512:640, :], hb[s, 640:768, :]], axis=1)
            half = dot(inter, both)
            for j in range(HALF // 128):
                k = low // 128 + j
                rows = slice(j * 128, (j + 1) * 128)
                weight = coef[k, pl.ds(s, 1), :]
                sall[k, :, columns] = inter[rows]
                hall[k, 0:128, columns] = (half[rows, 0:128] * weight).astype(BF16)
                hall[k, 128:256, columns] = (half[rows, 128:256] * weight).astype(BF16)

    def coefficients(ks):
        slots = lax.broadcasted_iota(jnp.int32, (16, 48), 0)
        zz, cc, pair = place(slots)
        position = ((zz * RING + x) * 2 + cc) * 2 + pair
        for k in ks:
            dx, p = pair_of_g(k)
            row = rg[dx, p:p + 1, :]
            weight = cg[dx, p:p + 1, :]
            picked = jnp.where(position == row, weight, 0.0)
            coef[k] = jnp.broadcast_to(jnp.sum(picked, axis=1, keepdims=True), (16, 128))

    build_at(0)
    build_at(1)
    for p in range(2):
        across = jnp.broadcast_to(en[p:p + 1, :], (128, 128))
        denom = across + jnp.transpose(across)
        amp = hb[p, 512:640, :].astype(F32)
        res = hb[p, 640:768, :].astype(F32)
        scale[p] = 0.5 / denom
        base[p, 0] = amp - 0.5 * (ex[p].astype(F32) + denom * amp) / denom
        base[p, 1] = res - 0.5 * (amp + denom * res) / denom
    for src, base_sem in ((cg, CG), (rg, RG)):
        arrive(src.at[3], base_sem + 3)
        send(src.at[3], src.at[2], base_sem + 2, up_x)
        arrive(src.at[1], base_sem + 1)
    tell(known.at[0], up_x, down_x)
    coefficients((0, 1, 2, 3, 4, 5))
    arrive_g(2)
    send_g(qg.at[2], 6, up_x)
    arrive_g(3)
    send_g(qg.at[3], 7, down_x)
    build_at(2)
    build_at(3)
    arrive_pair(2, 3)
    each(0, 2, lambda i: tile(i, 0))
    arrive_x(3, 0)
    send_x(3, 0, 2, up_y)
    arrive_x(1, 1)
    send_x(1, 1, 2, down_y)
    arrive_pair(4)
    send_part(4, 0, 12, up_z)
    send_part(4, 1, 12, up_z)
    send_pair(4, 6, sibling)
    arrive_pair(5)
    send_part(5, 0, 13, down_z)
    send_part(5, 1, 13, down_z)
    send_pair(5, 7, sibling)
    for src, base_sem in ((cg, CG), (rg, RG)):
        arrive(src.at[2], base_sem + 2)
    coefficients((6, 7))
    arrive_g(4, 5)
    build_at(4)
    build_at(5)
    arrive_pair(6, 7)
    each(2, 4, lambda i: tile(i, 0))
    pl.semaphore_wait(known.at[0], 2)
    tell(known.at[1], sibling)
    arrive_g(6, 7)
    build_at(6)
    build_at(7)
    arrive_pair(8)
    send_pair(8, 10, sibling)
    arrive_pair(9)
    send_pair(9, 11, sibling)
    each(0, 4, lambda i: tile(i, HALF))
    arrive_pair(10, 11)

    def whole(i):
        tile(i, 0)
        tile(i, HALF)

    each(4, 6, whole)
    pl.semaphore_wait(known.at[1], 1)
    tell(known.at[2], up_y, down_y)
    for part in range(2):
        for s in (12, 13):
            arrive_part(s, part)
            send_part(s, part, s + 2, sibling)
    each(6, 7, whole)
    for part in range(2):
        for s in (14, 15):
            arrive_part(s, part)
    each(7, 8, whole)

    def coupled(k):
        return dot_nt(hall[k], sall[k])

    def pass_on(i, value, where):
        rs_send[i] = value.astype(BF16)
        send(rs_send.at[i], rs_recv.at[i], RS + i, where)

    pass_on(0, coupled(6), up_x)
    pass_on(1, coupled(7), down_x)
    pass_on(2, coupled(3), up_x)
    pass_on(3, coupled(2), down_x)
    part0, part1 = coupled(5), coupled(4)
    arrive(rs_recv.at[0], RS + 0)
    pass_on(4, part0 + rs_recv[0].astype(F32), up_x)
    arrive(rs_recv.at[1], RS + 1)
    pass_on(5, part1 + rs_recv[1].astype(F32), down_x)
    pl.semaphore_wait(known.at[2], 2)
    tell(known.at[3], up_y, down_y)
    for d, half in ((3, 1), (1, 0), (2, 0), (2, 1)):
        arrive_x(d, half)

    def columns_of(j):
        s = (j // 2) * 4 + lax.rem(j, 2)
        theirs = domain_of(index_of(s))
        wide_rows = [
            jnp.concatenate([xall[d, theirs[b]] for d in range(RING)], axis=1) for b in range(4)
        ]
        rows = pl.ds(pl.multiple_of(j * 128, 128), 128)
        yall[rows, :] = dot_tn(hb[s, 0:512, :], jnp.concatenate(wide_rows, axis=0)).astype(BF16)
        for i in range(2):
            value = zero
            for b in range(4):
                value = lax.select(
                    theirs[b] == 2 * z + i, hb[s, b * 128:(b + 1) * 128, :], value
                )
            fsel[j, i * 128:(i + 1) * 128, :] = value

    each(0, 8, columns_of)
    own = [coupled(0), coupled(1)]
    def send_w(s, to, where):
        send(wb.at[s], wb.at[to], WB + to, where)

    for p in range(2):
        near, far = ((3, 4), (2, 5))[p]
        arrive(rs_recv.at[near], RS + near)
        arrive(rs_recv.at[far], RS + far)
        total = own[p] + rs_recv[near].astype(F32) + rs_recv[far].astype(F32)
        new_t = base[p, 0] - total[0:128] * scale[p]
        new_z = base[p, 1] - total[128:256] * scale[p]
        out_t[p] = new_t
        out_z[p] = new_z
        product = dot_nt(new_t.astype(BF16), new_z.astype(BF16))
        wb[p] = (0.5 * (product + jnp.transpose(product))).astype(BF16)
        send_w(p, (2, 4)[p], up_z)
        send_w(p, (5, 3)[p], down_z)
    pl.semaphore_wait(known.at[3], 2)

    def left_of(*js):
        for j in js:
            lall[:, j * 128:(j + 1) * 128] = dot(fsel[j], wb[j]).astype(BF16)

    left_of(0, 1)
    arrive(wb.at[2], WB + 2)
    send_w(2, 6, up_z)
    arrive(wb.at[3], WB + 3)
    send_w(3, 7, down_z)
    left_of(2, 3)
    for j in (4, 5):
        arrive(wb.at[j], WB + j)
    left_of(4, 5)
    early = dot(lall[:, 0:768], yall[0:768, :])
    for j in (6, 7):
        arrive(wb.at[j], WB + j)
    left_of(6, 7)

    def piece(i):
        dy, dx, dc = i // 8, (i // 2) % 4, i % 2
        return pltpu.make_async_remote_copy(
            src_ref=obuf.at[dy, lax.rem(x + dx, RING) * 2 + lax.rem(c + dc, 2)],
            dst_ref=rbuf.at[i], send_sem=send_sem.at[PIECE_SEND + i],
            recv_sem=recv_sem.at[PC + i], device_id=device(dx=dx, dc=dc, dy=dy),
            device_id_type=MESH,
        )

    pieces = [None] + [piece(i) for i in range(1, PIECES)]
    for dys in ((2, 3), (0, 1)):
        columns = slice(dys[0] * 128, dys[0] * 128 + 256)
        partial = early[:, columns] + dot(lall[:, 768:1024], yall[768:1024, columns])
        for d in dys:
            for i in range(8):
                block = partial[i * 32:(i + 1) * 32, (d - dys[0]) * 128:(d - dys[0] + 1) * 128]
                obuf[d, i] = block.astype(BF16)
        for d in dys:
            for i in (4, 5, 2, 3, 6, 7, 1, 0):
                if d * 8 + i:
                    pieces[d * 8 + i].start()
    for copy in sends:
        copy.wait_send()
    total = obuf[0, x * 2 + c].astype(F32)
    for i in range(1, PIECES):
        pieces[i].wait_recv()
        total = total + rbuf[i].astype(F32)
    out_r[...] = total
    for i in range(1, PIECES):
        pieces[i].wait_send()


def per_device(amps, resp, trans, ints, energies, couple, readers, domains, integrals):
    anywhere = pl.BlockSpec(memory_space=pltpu.HBM)
    vmem = pl.BlockSpec(memory_space=pltpu.VMEM)
    dma = pltpu.SemaphoreType.DMA
    return pl.pallas_call(
        kernel,
        out_shape=(
            jax.ShapeDtypeStruct((2, 128, 128), F32),
            jax.ShapeDtypeStruct((2, 128, 128), F32),
            jax.ShapeDtypeStruct((32, 128), F32),
        ),
        in_specs=[anywhere] * 9,
        out_specs=(vmem,) * 3,
        scratch_shapes=[
            pltpu.VMEM((16, 768, 128), BF16),
            pltpu.VMEM((8, 512, 128), BF16),
            pltpu.VMEM((8, 1024, 128), BF16),
            pltpu.VMEM((8, 128, 2048), BF16),
            pltpu.VMEM((8, 256, 2048), BF16),
            pltpu.VMEM((4, 8, 128, 128), BF16),
            pltpu.VMEM((1024, 512), BF16),
            pltpu.VMEM((8, 256, 128), BF16),
            pltpu.VMEM((256, 1024), BF16),
            pltpu.VMEM((8, 128, 128), BF16),
            pltpu.VMEM((8, 16, 128), F32),
            pltpu.VMEM((4, 2, 48), F32),
            pltpu.VMEM((4, 2, 48), jnp.int32),
            pltpu.SMEM((4, 256), jnp.int32),
            pltpu.VMEM((2, 128, 128), BF16),
            pltpu.VMEM((2, 128), F32),
            pltpu.VMEM((2, 2, 128, 128), F32),
            pltpu.VMEM((2, 128, 128), F32),
            pltpu.VMEM((6, 256, 128), BF16),
            pltpu.VMEM((6, 256, 128), BF16),
            pltpu.VMEM((4, 8, 32, 128), BF16),
            pltpu.VMEM((PIECES, 32, 128), BF16),
            dma((16,)), dma((N_SEND,)), dma((N_RECV,)), pltpu.SemaphoreType.REGULAR((4,)),
        ],
        compiler_params=pltpu.CompilerParams(
            collective_id=0, has_side_effects=True, vmem_limit_bytes=32 * 1024 * 1024
        ),
    )(
        *(
            pltpu.with_memory_space_constraint(value, pltpu.HBM)
            for value in (
                amps, resp, trans, ints, energies, couple, readers, domains.T,
                integrals.reshape(8, 128, 128),
            )
        )
    )


def solution(mesh):
    pairs3 = P(("wide", "narrow"), None, None)
    pairs2 = P(("wide", "narrow"), None)
    return jax.shard_map(
        per_device,
        mesh=mesh,
        in_specs=(
            pairs3, pairs3, pairs3, pairs3, pairs2, pairs2, pairs2, P(), P(None, "narrow"),
        ),
        out_specs=(pairs3, pairs3, P("wide", "narrow")),
        check_vma=False,
    )
```

```python
import jax
import jax.numpy as jnp
from jax import lax
from jax.experimental import pallas as pl
from jax.experimental.pallas import tpu as pltpu
from jax.sharding import PartitionSpec as P

MESH = pl.DeviceIdType.MESH
F32 = jnp.float32
BF16 = jnp.bfloat16
RING = 4
PIECES = 32
HALF = 512
G_PLACE = ((0, 0), (0, 1), (3, 0), (1, 1), (3, 1), (1, 0), (2, 0), (2, 1))

HB, HC, QG, CG, RG, XA, RS, WB, PC = 0, 16, 32, 40, 44, 48, 56, 62, 70
N_RECV = PC + PIECES
N_SEND = 140
PIECE_SEND = 104


def dot(a, b):
    return jnp.dot(a, b, preferred_element_type=F32)


def dot_nt(a, b):
    return lax.dot_general(a, b, (((1,), (1,)), ((), ())), preferred_element_type=F32)


def dot_tn(a, b):
    return lax.dot_general(a, b, (((0,), (0,)), ((), ())), preferred_element_type=F32)


def each(low, high, body):
    def step(i, carry):
        body(i)
        return carry
    lax.fori_loop(low, high, step, 0)


def kernel(
    amps, resp, trans, ints, energies, couple, readers, domains, integrals,
    out_t, out_z, out_r,
    hb, qg, at, sall, hall, xall, yall, fsel, lall, wb, coef, cg, rg, dom, ex, en,
    base, scale, rs_send, rs_recv, obuf, rbuf,
    local_sem, send_sem, recv_sem, known,
):
    wide = lax.axis_index("wide")
    y = lax.axis_index("narrow")
    c = lax.rem(wide, 2)
    x = lax.rem(wide // 2, RING)
    z = wide // (2 * RING)

    def device(dz=0, dx=0, dc=0, dy=0):
        zz, xx = lax.rem(z + dz, RING), lax.rem(x + dx, RING)
        return ((zz * RING + xx) * 2 + lax.rem(c + dc, 2), lax.rem(y + dy, RING))

    up_z, down_z = device(dz=1), device(dz=3)
    up_x, down_x = device(dx=1), device(dx=3)
    up_y, down_y = device(dy=1), device(dy=3)
    sibling = device(dc=1)

    def tell(sem, *where):
        for one in where:
            pl.semaphore_signal(sem, inc=1, device_id=one, device_id_type=MESH)

    barrier = pltpu.get_barrier_semaphore()
    tell(barrier, up_z, down_z, up_x, down_x, sibling, up_y, down_y)

    moves = []
    for p in range(2):
        moves += [
            (trans.at[p], hb.at[p, 0:512]), (amps.at[p], hb.at[p, 512:640]),
            (resp.at[p], hb.at[p, 640:768]),
        ]
    moves += [
        (couple, cg.at[0]), (readers, rg.at[0]), (integrals, xall.at[0]), (domains, dom),
        (ints, ex), (energies, en),
    ]
    copies = [
        pltpu.make_async_copy(src, dst, local_sem.at[i]) for i, (src, dst) in enumerate(moves)
    ]
    for copy in copies:
        copy.start()
    pl.semaphore_wait(barrier, 7)

    sends = []

    def send(src, dst, recv, where):
        copy = pltpu.make_async_remote_copy(
            src_ref=src, dst_ref=dst, send_sem=send_sem.at[len(sends)],
            recv_sem=recv_sem.at[recv], device_id=where, device_id_type=MESH,
        )
        sends.append(copy)
        copy.start()

    def arrive(ref, recv):
        pltpu.make_async_remote_copy(
            src_ref=ref, dst_ref=ref, send_sem=send_sem.at[0],
            recv_sem=recv_sem.at[recv], device_id=sibling, device_id_type=MESH,
        ).wait_recv()

    def send_pair(s, to, where):
        send(hb.at[s], hb.at[to], HB + to, where)

    def arrive_pair(*slots):
        for s in slots:
            arrive(hb.at[s], HB + s)

    PARTS = ((slice(0, 384), HB), (slice(384, 768), HC))

    def send_part(s, part, to, where):
        rows, sem = PARTS[part]
        send(hb.at[s, rows], hb.at[to, rows], sem + to, where)

    def arrive_part(s, part):
        rows, sem = PARTS[part]
        arrive(hb.at[s, rows], sem + s)

    def send_g(src, to, where):
        send(src, qg.at[to], QG + to, where)

    def arrive_g(*slots):
        for s in slots:
            arrive(qg.at[s], QG + s)

    def send_x(d, half, to, where):
        rows = slice(half * 4, half * 4 + 4)
        send(xall.at[d, rows], xall.at[to, rows], XA + to * 2 + half, where)

    def arrive_x(d, half):
        arrive(xall.at[d, half * 4:half * 4 + 4], XA + d * 2 + half)

    def send_own(p, to, where):
        send(trans.at[p], hb.at[to, 0:512], HB + to, where)
        send(amps.at[p], hb.at[to, 512:640], HB + to, where)
        send(resp.at[p], hb.at[to, 640:768], HB + to, where)

    send_own(0, 4, up_z)
    send_own(1, 5, down_z)
    send_g(trans.at[0], 2, up_x)
    send_g(trans.at[1], 3, down_x)
    send_own(0, 2, sibling)
    send_own(1, 3, sibling)
    send_own(1, 8, up_z)
    send_own(0, 9, down_z)
    send_g(trans.at[1], 4, up_x)
    send_g(trans.at[0], 5, down_x)
    for src, dst, base_sem in ((couple, cg, CG), (readers, rg, RG)):
        send(src, dst.at[3], base_sem + 3, up_x)
        send(src, dst.at[1], base_sem + 1, down_x)
    for half, to, where in ((0, 3, up_y), (1, 1, down_y), (1, 3, up_y), (0, 1, down_y)):
        rows = slice(half * 4, half * 4 + 4)
        send(integrals.at[rows], xall.at[to, rows], XA + to * 2 + half, where)
    for copy in copies:
        copy.wait()

    def domain_of(index):
        return [dom[a, index] for a in range(4)]

    zero = jnp.zeros((128, 128), BF16)

    def pair_of_g(k):
        return G_PLACE[k]

    def build_at(k):
        dx, pair = pair_of_g(k)
        own = domain_of((((z * RING + lax.rem(x + dx, RING)) * 2 + c) * RING + y) * 2 + pair)
        source = hb if k < 2 else qg
        turned = [jnp.transpose(source[k, a * 128:(a + 1) * 128, :]) for a in range(4)]
        for block in range(8):
            value = zero
            for a in range(4):
                value = lax.select(own[a] == block, turned[a], value)
            at[block, k * 128:(k + 1) * 128, :] = value

    def place(s):
        group, inner = s // 4, lax.rem(s, 4)
        flip, i = inner // 2, lax.rem(inner, 2)
        near = jnp.where(i == 0, 3, 1)
        dz = jnp.where(group == 0, 0, jnp.where(group == 3, 2, near))
        pair = jnp.where(group == 2, 1 - i, i)
        return lax.rem(z + dz, RING), lax.rem(c + flip, 2), pair

    def index_of(s):
        zz, cc, pair = place(s)
        return (((zz * RING + x) * 2 + cc) * RING + y) * 2 + pair

    def tile(i, low):
        pair = (2 * i, 2 * i + 1)
        inters = []
        for s in pair:
            theirs = domain_of(index_of(s))
            left = jnp.concatenate([at[theirs[b], low:low + HALF, :] for b in range(4)], axis=1)
            inters.append(dot(left, hb[s, 0:512, :]).astype(BF16))
        for s, inter in zip(pair, inters):
            columns = pl.ds(pl.multiple_of(s * 128, 128), 128)
            both = jnp.concatenate([hb[s, 512:640, :], hb[s, 640:768, :]], axis=1)
            half = dot(inter, both)
            for j in range(HALF // 128):
                k = low // 128 + j
                rows = slice(j * 128, (j + 1) * 128)
                weight = coef[k, pl.ds(s, 1), :]
                sall[k, :, columns] = inter[rows]
                hall[k, 0:128, columns] = (half[rows, 0:128] * weight).astype(BF16)
                hall[k, 128:256, columns] = (half[rows, 128:256] * weight).astype(BF16)

    def coefficients(ks):
        slots = lax.broadcasted_iota(jnp.int32, (16, 48), 0)
        zz, cc, pair = place(slots)
        position = ((zz * RING + x) * 2 + cc) * 2 + pair
        for k in ks:
            dx, p = pair_of_g(k)
            row = rg[dx, p:p + 1, :]
            weight = cg[dx, p:p + 1, :]
            picked = jnp.where(position == row, weight, 0.0)
            coef[k] = jnp.broadcast_to(jnp.sum(picked, axis=1, keepdims=True), (16, 128))

    build_at(0)
    build_at(1)
    for p in range(2):
        across = jnp.broadcast_to(en[p:p + 1, :], (128, 128))
        denom = across + jnp.transpose(across)
        amp = hb[p, 512:640, :].astype(F32)
        res = hb[p, 640:768, :].astype(F32)
        scale[p] = 0.5 / denom
        base[p, 0] = amp - 0.5 * (ex[p].astype(F32) + denom * amp) / denom
        base[p, 1] = res - 0.5 * (amp + denom * res) / denom
    for src, base_sem in ((cg, CG), (rg, RG)):
        arrive(src.at[3], base_sem + 3)
        send(src.at[3], src.at[2], base_sem + 2, up_x)
        arrive(src.at[1], base_sem + 1)
    tell(known.at[0], up_x, down_x)
    coefficients((0, 1, 2, 3, 4, 5))
    arrive_g(2)
    send_g(qg.at[2], 6, up_x)
    arrive_g(3)
    send_g(qg.at[3], 7, down_x)
    build_at(2)
    build_at(3)
    arrive_pair(2, 3)
    each(0, 2, lambda i: tile(i, 0))
    arrive_x(3, 0)
    send_x(3, 0, 2, up_y)
    arrive_x(1, 1)
    send_x(1, 1, 2, down_y)
    arrive_pair(4)
    send_part(4, 0, 12, up_z)
    send_part(4, 1, 12, up_z)
    send_pair(4, 6, sibling)
    arrive_pair(5)
    send_part(5, 0, 13, down_z)
    send_part(5, 1, 13, down_z)
    send_pair(5, 7, sibling)
    for src, base_sem in ((cg, CG), (rg, RG)):
        arrive(src.at[2], base_sem + 2)
    coefficients((6, 7))
    arrive_g(4, 5)
    build_at(4)
    build_at(5)
    arrive_pair(6, 7)
    each(2, 4, lambda i: tile(i, 0))
    pl.semaphore_wait(known.at[0], 2)
    tell(known.at[1], sibling)
    arrive_g(6, 7)
    build_at(6)
    build_at(7)
    arrive_pair(8)
    send_pair(8, 10, sibling)
    arrive_pair(9)
    send_pair(9, 11, sibling)
    each(0, 4, lambda i: tile(i, HALF))
    arrive_pair(10, 11)

    def whole(i):
        tile(i, 0)
        tile(i, HALF)

    each(4, 6, whole)
    pl.semaphore_wait(known.at[1], 1)
    tell(known.at[2], up_y, down_y)
    for part in range(2):
        for s in (12, 13):
            arrive_part(s, part)
            send_part(s, part, s + 2, sibling)
    each(6, 7, whole)
    for part in range(2):
        for s in (14, 15):
            arrive_part(s, part)
    each(7, 8, whole)

    def coupled(k):
        return dot_nt(hall[k], sall[k])

    for ks in ((6,), (5, 2), (7,), (3, 4)):
        values = [coupled(k) for k in ks]
        for k, value in zip(ks, values):
            dx, p = G_PLACE[k]
            i = dx * 2 - 2 + p
            rs_send[i] = value.astype(BF16)
            send(rs_send.at[i], rs_recv.at[i], RS + i, device(dx=dx))
    pl.semaphore_wait(known.at[2], 2)
    tell(known.at[3], up_y, down_y)
    for d, half in ((3, 1), (1, 0), (2, 0), (2, 1)):
        arrive_x(d, half)

    def columns_of(j):
        p, r = j // 4, lax.rem(j, 4)
        near = jnp.where(r == 1, 4 + 4 * p, 9 - 4 * p)
        s = jnp.where(r == 0, p, jnp.where(r == 3, 12 + p, near))
        theirs = domain_of(index_of(s))
        wide_rows = [
            jnp.concatenate([xall[d, theirs[b]] for d in range(RING)], axis=1) for b in range(4)
        ]
        rows = pl.ds(pl.multiple_of(j * 128, 128), 128)
        yall[rows, :] = dot_tn(hb[s, 0:512, :], jnp.concatenate(wide_rows, axis=0)).astype(BF16)
        for i in range(2):
            value = zero
            for b in range(4):
                value = lax.select(
                    theirs[b] == 2 * z + i, hb[s, b * 128:(b + 1) * 128, :], value
                )
            fsel[j, i * 128:(i + 1) * 128, :] = value

    each(0, 8, columns_of)
    own = [coupled(0), coupled(1)]
    def send_w(s, to, where):
        send(wb.at[s], wb.at[to], WB + to, where)

    for p in range(2):
        total = own[p]
        for i in (p, 4 + p, 2 + p):
            arrive(rs_recv.at[i], RS + i)
            total = total + rs_recv[i].astype(F32)
        new_t = base[p, 0] - total[0:128] * scale[p]
        new_z = base[p, 1] - total[128:256] * scale[p]
        out_t[p] = new_t
        out_z[p] = new_z
        product = dot_nt(new_t.astype(BF16), new_z.astype(BF16))
        wb[p * 4] = (0.5 * (product + jnp.transpose(product))).astype(BF16)
        send_w(p * 4, p * 4 + 3, device(dz=2))
        send_w(p * 4, p * 4 + 1, up_z)
        send_w(p * 4, p * 4 + 2, down_z)
    pl.semaphore_wait(known.at[3], 2)

    def left_of(*js):
        for j in js:
            lall[:, j * 128:(j + 1) * 128] = dot(fsel[j], wb[j]).astype(BF16)

    left_of(0, 4)
    for j in (1, 2, 3):
        arrive(wb.at[j], WB + j)
    left_of(1, 2, 3)
    early = dot(lall[:, 0:512], yall[0:512, :])
    for j in (5, 6, 7):
        arrive(wb.at[j], WB + j)
    left_of(5, 6, 7)

    def piece(i):
        dy, dx, dc = i // 8, (i // 2) % 4, i % 2
        return pltpu.make_async_remote_copy(
            src_ref=obuf.at[dy, lax.rem(x + dx, RING) * 2 + lax.rem(c + dc, 2)],
            dst_ref=rbuf.at[i], send_sem=send_sem.at[PIECE_SEND + i],
            recv_sem=recv_sem.at[PC + i], device_id=device(dx=dx, dc=dc, dy=dy),
            device_id_type=MESH,
        )

    pieces = [None] + [piece(i) for i in range(1, PIECES)]
    for dys in ((2, 3), (0, 1)):
        columns = slice(dys[0] * 128, dys[0] * 128 + 256)
        partial = early[:, columns] + dot(lall[:, 512:1024], yall[512:1024, columns])
        for d in dys:
            for i in range(8):
                block = partial[i * 32:(i + 1) * 32, (d - dys[0]) * 128:(d - dys[0] + 1) * 128]
                obuf[d, i] = block.astype(BF16)
        for d in dys:
            for i in (4, 5, 2, 3, 6, 7, 1, 0):
                if d * 8 + i:
                    pieces[d * 8 + i].start()
    for copy in sends:
        copy.wait_send()
    total = obuf[0, x * 2 + c].astype(F32)
    for i in range(1, PIECES):
        pieces[i].wait_recv()
        total = total + rbuf[i].astype(F32)
    out_r[...] = total
    for i in range(1, PIECES):
        pieces[i].wait_send()


def per_device(amps, resp, trans, ints, energies, couple, readers, domains, integrals):
    anywhere = pl.BlockSpec(memory_space=pltpu.HBM)
    vmem = pl.BlockSpec(memory_space=pltpu.VMEM)
    dma = pltpu.SemaphoreType.DMA
    return pl.pallas_call(
        kernel,
        out_shape=(
            jax.ShapeDtypeStruct((2, 128, 128), F32),
            jax.ShapeDtypeStruct((2, 128, 128), F32),
            jax.ShapeDtypeStruct((32, 128), F32),
        ),
        in_specs=[anywhere] * 9,
        out_specs=(vmem,) * 3,
        scratch_shapes=[
            pltpu.VMEM((16, 768, 128), BF16),
            pltpu.VMEM((8, 512, 128), BF16),
            pltpu.VMEM((8, 1024, 128), BF16),
            pltpu.VMEM((8, 128, 2048), BF16),
            pltpu.VMEM((8, 256, 2048), BF16),
            pltpu.VMEM((4, 8, 128, 128), BF16),
            pltpu.VMEM((1024, 512), BF16),
            pltpu.VMEM((8, 256, 128), BF16),
            pltpu.VMEM((256, 1024), BF16),
            pltpu.VMEM((8, 128, 128), BF16),
            pltpu.VMEM((8, 16, 128), F32),
            pltpu.VMEM((4, 2, 48), F32),
            pltpu.VMEM((4, 2, 48), jnp.int32),
            pltpu.SMEM((4, 256), jnp.int32),
            pltpu.VMEM((2, 128, 128), BF16),
            pltpu.VMEM((2, 128), F32),
            pltpu.VMEM((2, 2, 128, 128), F32),
            pltpu.VMEM((2, 128, 128), F32),
            pltpu.VMEM((6, 256, 128), BF16),
            pltpu.VMEM((6, 256, 128), BF16),
            pltpu.VMEM((4, 8, 32, 128), BF16),
            pltpu.VMEM((PIECES, 32, 128), BF16),
            dma((16,)), dma((N_SEND,)), dma((N_RECV,)), pltpu.SemaphoreType.REGULAR((4,)),
        ],
        compiler_params=pltpu.CompilerParams(
            collective_id=0, has_side_effects=True, vmem_limit_bytes=32 * 1024 * 1024
        ),
    )(
        *(
            pltpu.with_memory_space_constraint(value, pltpu.HBM)
            for value in (
                amps, resp, trans, ints, energies, couple, readers, domains.T,
                integrals.reshape(8, 128, 128),
            )
        )
    )


def solution(mesh):
    pairs3 = P(("wide", "narrow"), None, None)
    pairs2 = P(("wide", "narrow"), None)
    return jax.shard_map(
        per_device,
        mesh=mesh,
        in_specs=(
            pairs3, pairs3, pairs3, pairs3, pairs2, pairs2, pairs2, P(), P(None, "narrow"),
        ),
        out_specs=(pairs3, pairs3, P("wide", "narrow")),
        check_vma=False,
    )
```

```python
import jax
import jax.numpy as jnp
from jax import lax
from jax.experimental import pallas as pl
from jax.experimental.pallas import tpu as pltpu
from jax.sharding import PartitionSpec as P

MESH = pl.DeviceIdType.MESH
F32 = jnp.float32
BF16 = jnp.bfloat16
RING = 4
PIECES = 32
HALF = 512
G_PLACE = ((0, 0), (0, 1), (3, 0), (1, 1), (3, 1), (1, 0), (2, 0), (2, 1))

HB, HC, QG, CG, RG, XA, RS, WB, PC = 0, 16, 32, 40, 44, 48, 56, 62, 70
N_RECV = PC + PIECES
N_SEND = 140
PIECE_SEND = 104


def dot(a, b):
    return jnp.dot(a, b, preferred_element_type=F32)


def dot_nt(a, b):
    return lax.dot_general(a, b, (((1,), (1,)), ((), ())), preferred_element_type=F32)


def dot_tn(a, b):
    return lax.dot_general(a, b, (((0,), (0,)), ((), ())), preferred_element_type=F32)


def each(low, high, body):
    def step(i, carry):
        body(i)
        return carry
    lax.fori_loop(low, high, step, 0)


def kernel(
    amps, resp, trans, ints, energies, couple, readers, domains, integrals,
    out,
    hb, qg, at, sall, hall, xall, yall, fsel, lall, wb, coef, cg, rg, dom, ex, en,
    base, scale, rs_send, rs_recv, obuf, rbuf,
    local_sem, send_sem, recv_sem, known,
):
    wide = lax.axis_index("wide")
    y = lax.axis_index("narrow")
    c = lax.rem(wide, 2)
    x = lax.rem(wide // 2, RING)
    z = wide // (2 * RING)

    def device(dz=0, dx=0, dc=0, dy=0):
        zz, xx = lax.rem(z + dz, RING), lax.rem(x + dx, RING)
        return ((zz * RING + xx) * 2 + lax.rem(c + dc, 2), lax.rem(y + dy, RING))

    up_z, down_z = device(dz=1), device(dz=3)
    up_x, down_x = device(dx=1), device(dx=3)
    up_y, down_y = device(dy=1), device(dy=3)
    sibling = device(dc=1)

    def tell(sem, *where):
        for one in where:
            pl.semaphore_signal(sem, inc=1, device_id=one, device_id_type=MESH)

    barrier = pltpu.get_barrier_semaphore()
    tell(barrier, up_z, down_z, up_x, down_x, sibling, up_y, down_y)

    moves = []
    for p in range(2):
        moves += [
            (trans.at[p], hb.at[p, 0:512]), (amps.at[p], hb.at[p, 512:640]),
            (resp.at[p], hb.at[p, 640:768]),
        ]
    moves += [
        (couple, cg.at[0]), (readers, rg.at[0]), (integrals, xall.at[0]), (domains, dom),
        (ints, ex), (energies, en),
    ]
    copies = [
        pltpu.make_async_copy(src, dst, local_sem.at[i]) for i, (src, dst) in enumerate(moves)
    ]
    for copy in copies:
        copy.start()
    pl.semaphore_wait(barrier, 7)

    sends = []

    def send(src, dst, recv, where):
        copy = pltpu.make_async_remote_copy(
            src_ref=src, dst_ref=dst, send_sem=send_sem.at[len(sends)],
            recv_sem=recv_sem.at[recv], device_id=where, device_id_type=MESH,
        )
        sends.append(copy)
        copy.start()

    def arrive(ref, recv):
        pltpu.make_async_remote_copy(
            src_ref=ref, dst_ref=ref, send_sem=send_sem.at[0],
            recv_sem=recv_sem.at[recv], device_id=sibling, device_id_type=MESH,
        ).wait_recv()

    def send_pair(s, to, where):
        send(hb.at[s], hb.at[to], HB + to, where)

    def arrive_pair(*slots):
        for s in slots:
            arrive(hb.at[s], HB + s)

    PARTS = ((slice(0, 384), HB), (slice(384, 768), HC))

    def send_part(s, part, to, where):
        rows, sem = PARTS[part]
        send(hb.at[s, rows], hb.at[to, rows], sem + to, where)

    def arrive_part(s, part):
        rows, sem = PARTS[part]
        arrive(hb.at[s, rows], sem + s)

    def send_g(src, to, where):
        send(src, qg.at[to], QG + to, where)

    def arrive_g(*slots):
        for s in slots:
            arrive(qg.at[s], QG + s)

    def send_x(d, half, to, where):
        rows = slice(half * 4, half * 4 + 4)
        send(xall.at[d, rows], xall.at[to, rows], XA + to * 2 + half, where)

    def arrive_x(d, half):
        arrive(xall.at[d, half * 4:half * 4 + 4], XA + d * 2 + half)

    def send_own(p, to, where):
        send(trans.at[p], hb.at[to, 0:512], HB + to, where)
        send(amps.at[p], hb.at[to, 512:640], HB + to, where)
        send(resp.at[p], hb.at[to, 640:768], HB + to, where)

    for src, dst, base_sem in ((couple, cg, CG), (readers, rg, RG)):
        send(src, dst.at[3], base_sem + 3, up_x)
        send(src, dst.at[1], base_sem + 1, down_x)
    send_own(0, 4, up_z)
    send_own(1, 5, down_z)
    send_g(trans.at[0], 2, up_x)
    send_g(trans.at[1], 3, down_x)
    send_own(0, 2, sibling)
    send_own(1, 3, sibling)
    send_own(1, 8, up_z)
    send_own(0, 9, down_z)
    send_g(trans.at[1], 4, up_x)
    send_g(trans.at[0], 5, down_x)
    for half, to, where in ((0, 3, up_y), (1, 1, down_y), (1, 3, up_y), (0, 1, down_y)):
        rows = slice(half * 4, half * 4 + 4)
        send(integrals.at[rows], xall.at[to, rows], XA + to * 2 + half, where)
    for copy in copies:
        copy.wait()

    def domain_of(index):
        return [dom[a, index] for a in range(4)]

    zero = jnp.zeros((128, 128), BF16)

    def pair_of_g(k):
        return G_PLACE[k]

    def build_at(k):
        dx, pair = pair_of_g(k)
        own = domain_of((((z * RING + lax.rem(x + dx, RING)) * 2 + c) * RING + y) * 2 + pair)
        source = hb if k < 2 else qg
        turned = [jnp.transpose(source[k, a * 128:(a + 1) * 128, :]) for a in range(4)]
        for block in range(8):
            value = zero
            for a in range(4):
                value = lax.select(own[a] == block, turned[a], value)
            at[block, k * 128:(k + 1) * 128, :] = value

    def place(s):
        group, inner = s // 4, lax.rem(s, 4)
        flip, i = inner // 2, lax.rem(inner, 2)
        near = jnp.where(i == 0, 3, 1)
        dz = jnp.where(group == 0, 0, jnp.where(group == 3, 2, near))
        pair = jnp.where(group == 2, 1 - i, i)
        return lax.rem(z + dz, RING), lax.rem(c + flip, 2), pair

    def index_of(s):
        zz, cc, pair = place(s)
        return (((zz * RING + x) * 2 + cc) * RING + y) * 2 + pair

    def tile(i, low, size=HALF):
        pair = (2 * i, 2 * i + 1)
        inters = []
        for s in pair:
            theirs = domain_of(index_of(s))
            left = jnp.concatenate([at[theirs[b], low:low + size, :] for b in range(4)], axis=1)
            inters.append(dot(left, hb[s, 0:512, :]).astype(BF16))
        for s, inter in zip(pair, inters):
            columns = pl.ds(pl.multiple_of(s * 128, 128), 128)
            both = jnp.concatenate([hb[s, 512:640, :], hb[s, 640:768, :]], axis=1)
            half = dot(inter, both)
            for j in range(size // 128):
                k = low // 128 + j
                rows = slice(j * 128, (j + 1) * 128)
                weight = coef[k, pl.ds(s, 1), :]
                sall[k, :, columns] = inter[rows]
                hall[k, 0:128, columns] = (half[rows, 0:128] * weight).astype(BF16)
                hall[k, 128:256, columns] = (half[rows, 128:256] * weight).astype(BF16)

    def coefficients(ks):
        slots = lax.broadcasted_iota(jnp.int32, (16, 48), 0)
        zz, cc, pair = place(slots)
        position = ((zz * RING + x) * 2 + cc) * 2 + pair
        for k in ks:
            dx, p = pair_of_g(k)
            row = rg[dx, p:p + 1, :]
            weight = cg[dx, p:p + 1, :]
            picked = jnp.where(position == row, weight, 0.0)
            coef[k] = jnp.broadcast_to(jnp.sum(picked, axis=1, keepdims=True), (16, 128))

    build_at(0)
    build_at(1)
    for p in range(2):
        across = jnp.broadcast_to(en[p:p + 1, :], (128, 128))
        denom = across + jnp.transpose(across)
        amp = hb[p, 512:640, :].astype(F32)
        res = hb[p, 640:768, :].astype(F32)
        scale[p] = 0.5 / denom
        base[p, 0] = amp - 0.5 * (ex[p].astype(F32) + denom * amp) / denom
        base[p, 1] = res - 0.5 * (amp + denom * res) / denom
    for src, base_sem in ((cg, CG), (rg, RG)):
        arrive(src.at[3], base_sem + 3)
        send(src.at[3], src.at[2], base_sem + 2, up_x)
        arrive(src.at[1], base_sem + 1)
    tell(known.at[0], up_x, down_x)
    coefficients((0, 1, 2, 3, 4, 5))
    arrive_g(2)
    send_g(qg.at[2], 6, up_x)
    arrive_g(3)
    send_g(qg.at[3], 7, down_x)
    build_at(2)
    build_at(3)
    arrive_pair(2, 3)
    each(0, 2, lambda i: tile(i, 0))
    arrive_x(3, 0)
    send_x(3, 0, 2, up_y)
    arrive_x(1, 1)
    send_x(1, 1, 2, down_y)
    arrive_pair(4)
    send_part(4, 0, 12, up_z)
    send_part(4, 1, 12, up_z)
    send_pair(4, 6, sibling)
    arrive_pair(5)
    send_part(5, 0, 13, down_z)
    send_part(5, 1, 13, down_z)
    send_pair(5, 7, sibling)
    for src, base_sem in ((cg, CG), (rg, RG)):
        arrive(src.at[2], base_sem + 2)
    coefficients((6, 7))
    arrive_g(4, 5)
    build_at(4)
    build_at(5)
    arrive_pair(6, 7)
    each(2, 4, lambda i: tile(i, 0))
    each(0, 4, lambda i: tile(i, HALF, HALF // 2))
    pl.semaphore_wait(known.at[0], 2)
    tell(known.at[1], sibling)
    arrive_g(6, 7)
    build_at(6)
    build_at(7)
    arrive_pair(8)
    send_pair(8, 10, sibling)
    arrive_pair(9)
    send_pair(9, 11, sibling)
    each(0, 4, lambda i: tile(i, HALF + HALF // 2, HALF // 2))
    arrive_pair(10, 11)

    def whole(i):
        tile(i, 0)
        tile(i, HALF)

    each(4, 6, whole)
    pl.semaphore_wait(known.at[1], 1)
    tell(known.at[2], up_y, down_y)
    for part in range(2):
        for s in (12, 13):
            arrive_part(s, part)
            send_part(s, part, s + 2, sibling)
    each(6, 7, whole)
    for part in range(2):
        for s in (14, 15):
            arrive_part(s, part)
    each(7, 8, whole)

    def coupled(k):
        return dot_nt(hall[k], sall[k])

    for ks in ((6,), (5, 2), (7,), (3, 4)):
        values = [coupled(k) for k in ks]
        for k, value in zip(ks, values):
            dx, p = G_PLACE[k]
            i = dx * 2 - 2 + p
            rs_send[i] = value.astype(BF16)
            send(rs_send.at[i], rs_recv.at[i], RS + i, device(dx=dx))
    pl.semaphore_wait(known.at[2], 2)
    tell(known.at[3], up_y, down_y)
    for d, half in ((3, 1), (1, 0), (2, 0), (2, 1)):
        arrive_x(d, half)

    def columns_of(j):
        p, r = j // 4, lax.rem(j, 4)
        near = jnp.where(r == 1, 4 + 4 * p, 9 - 4 * p)
        s = jnp.where(r == 0, p, jnp.where(r == 3, 12 + p, near))
        theirs = domain_of(index_of(s))
        wide_rows = [
            jnp.concatenate([xall[d, theirs[b]] for d in range(RING)], axis=1) for b in range(4)
        ]
        rows = pl.ds(pl.multiple_of(j * 128, 128), 128)
        yall[rows, :] = dot_tn(hb[s, 0:512, :], jnp.concatenate(wide_rows, axis=0)).astype(BF16)
        for i in range(2):
            value = zero
            for b in range(4):
                value = lax.select(
                    theirs[b] == 2 * z + i, hb[s, b * 128:(b + 1) * 128, :], value
                )
            fsel[j, i * 128:(i + 1) * 128, :] = value

    each(0, 4, columns_of)
    def send_w(s, to, where):
        send(wb.at[s], wb.at[to], WB + to, where)

    for p in range(2):
        total = coupled(p)
        for i in (p, 4 + p, 2 + p):
            arrive(rs_recv.at[i], RS + i)
            total = total + rs_recv[i].astype(F32)
        new_t = base[p, 0] - total[0:128] * scale[p]
        new_z = base[p, 1] - total[128:256] * scale[p]
        out[p * 128:(p + 1) * 128] = new_t
        out[256 + p * 128:384 + p * 128] = new_z
        product = dot_nt(new_t.astype(BF16), new_z.astype(BF16))
        wb[p * 4] = (0.5 * (product + jnp.transpose(product))).astype(BF16)
        send_w(p * 4, p * 4 + 3, device(dz=2))
        send_w(p * 4, p * 4 + 1, up_z)
        send_w(p * 4, p * 4 + 2, down_z)
    pl.semaphore_wait(known.at[3], 2)

    def left_of(*js):
        for j in js:
            lall[:, j * 128:(j + 1) * 128] = dot(fsel[j], wb[j]).astype(BF16)

    each(4, 8, columns_of)
    left_of(0, 4)
    for j in (1, 2, 3):
        arrive(wb.at[j], WB + j)
    left_of(1, 2, 3)
    early = dot(lall[:, 0:512], yall[0:512, :])
    for j in (5, 6, 7):
        arrive(wb.at[j], WB + j)
    left_of(5, 6, 7)

    def piece(i):
        dy, dx, dc = i // 8, (i // 2) % 4, i % 2
        return pltpu.make_async_remote_copy(
            src_ref=obuf.at[dy, lax.rem(x + dx, RING) * 2 + lax.rem(c + dc, 2)],
            dst_ref=rbuf.at[i], send_sem=send_sem.at[PIECE_SEND + i],
            recv_sem=recv_sem.at[PC + i], device_id=device(dx=dx, dc=dc, dy=dy),
            device_id_type=MESH,
        )

    pieces = [None] + [piece(i) for i in range(1, PIECES)]
    for dys in ((2, 3), (0, 1)):
        columns = slice(dys[0] * 128, dys[0] * 128 + 256)
        partial = early[:, columns] + dot(lall[:, 512:1024], yall[512:1024, columns])
        for d in dys:
            for i in range(8):
                block = partial[i * 32:(i + 1) * 32, (d - dys[0]) * 128:(d - dys[0] + 1) * 128]
                obuf[d, i] = block.astype(BF16)
        for d in dys:
            for i in (4, 5, 2, 3, 6, 7, 1, 0):
                if d * 8 + i:
                    pieces[d * 8 + i].start()
    for copy in sends:
        copy.wait_send()
    total = obuf[0, x * 2 + c].astype(F32)
    for i in range(1, PIECES):
        pieces[i].wait_recv()
        total = total + rbuf[i].astype(F32)
    out[512:544] = total
    for i in range(1, PIECES):
        pieces[i].wait_send()


def per_device(amps, resp, trans, ints, energies, couple, readers, domains, integrals):
    anywhere = pl.BlockSpec(memory_space=pltpu.HBM)
    vmem = pl.BlockSpec(memory_space=pltpu.VMEM)
    dma = pltpu.SemaphoreType.DMA
    out = pl.pallas_call(
        kernel,
        out_shape=jax.ShapeDtypeStruct((544, 128), F32),
        in_specs=[anywhere] * 9,
        out_specs=vmem,
        scratch_shapes=[
            pltpu.VMEM((16, 768, 128), BF16),
            pltpu.VMEM((8, 512, 128), BF16),
            pltpu.VMEM((8, 1024, 128), BF16),
            pltpu.VMEM((8, 128, 2048), BF16),
            pltpu.VMEM((8, 256, 2048), BF16),
            pltpu.VMEM((4, 8, 128, 128), BF16),
            pltpu.VMEM((1024, 512), BF16),
            pltpu.VMEM((8, 256, 128), BF16),
            pltpu.VMEM((256, 1024), BF16),
            pltpu.VMEM((8, 128, 128), BF16),
            pltpu.VMEM((8, 16, 128), F32),
            pltpu.VMEM((4, 2, 48), F32),
            pltpu.VMEM((4, 2, 48), jnp.int32),
            pltpu.SMEM((4, 256), jnp.int32),
            pltpu.VMEM((2, 128, 128), BF16),
            pltpu.VMEM((2, 128), F32),
            pltpu.VMEM((2, 2, 128, 128), F32),
            pltpu.VMEM((2, 128, 128), F32),
            pltpu.VMEM((6, 256, 128), BF16),
            pltpu.VMEM((6, 256, 128), BF16),
            pltpu.VMEM((4, 8, 32, 128), BF16),
            pltpu.VMEM((PIECES, 32, 128), BF16),
            dma((16,)), dma((N_SEND,)), dma((N_RECV,)), pltpu.SemaphoreType.REGULAR((4,)),
        ],
        compiler_params=pltpu.CompilerParams(
            collective_id=0, has_side_effects=True, vmem_limit_bytes=32 * 1024 * 1024
        ),
    )(
        *(
            pltpu.with_memory_space_constraint(value, pltpu.HBM)
            for value in (
                amps, resp, trans, ints, energies, couple, readers, domains.T,
                integrals.reshape(8, 128, 128),
            )
        )
    )
    return (
        out[0:256].reshape(2, 128, 128), out[256:512].reshape(2, 128, 128), out[512:544],
    )


def solution(mesh):
    pairs3 = P(("wide", "narrow"), None, None)
    pairs2 = P(("wide", "narrow"), None)
    return jax.shard_map(
        per_device,
        mesh=mesh,
        in_specs=(
            pairs3, pairs3, pairs3, pairs3, pairs2, pairs2, pairs2, P(), P(None, "narrow"),
        ),
        out_specs=(pairs3, pairs3, P("wide", "narrow")),
        check_vma=False,
    )
```

```python
import jax
import jax.numpy as jnp
from jax import lax
from jax.experimental import pallas as pl
from jax.experimental.pallas import tpu as pltpu
from jax.sharding import PartitionSpec as P

MESH = pl.DeviceIdType.MESH
F32 = jnp.float32
BF16 = jnp.bfloat16
RING = 4
PIECES = 32
HALF = 512
G_PLACE = ((0, 0), (0, 1), (3, 0), (1, 1), (3, 1), (1, 0), (2, 0), (2, 1))

HB, HC, QG, CG, RG, XA, RS, WB, PC = 0, 16, 32, 40, 44, 48, 56, 62, 70
N_RECV = PC + PIECES
N_SEND = 140
PIECE_SEND = 104


def dot(a, b):
    return jnp.dot(a, b, preferred_element_type=F32)


def dot_nt(a, b):
    return lax.dot_general(a, b, (((1,), (1,)), ((), ())), preferred_element_type=F32)


def dot_tn(a, b):
    return lax.dot_general(a, b, (((0,), (0,)), ((), ())), preferred_element_type=F32)


def each(low, high, body):
    def step(i, carry):
        body(i)
        return carry
    lax.fori_loop(low, high, step, 0)


def kernel(
    amps, resp, trans, ints, energies, couple, readers, domains, integrals,
    out,
    hb, qg, at, sall, hall, xall, yall, fsel, lall, wb, coef, cg, rg, dom, ex, en,
    base, scale, rs_send, rs_recv, obuf, rbuf,
    local_sem, send_sem, recv_sem, known,
):
    wide = lax.axis_index("wide")
    y = lax.axis_index("narrow")
    c = lax.rem(wide, 2)
    x = lax.rem(wide // 2, RING)
    z = wide // (2 * RING)

    def device(dz=0, dx=0, dc=0, dy=0):
        zz, xx = lax.rem(z + dz, RING), lax.rem(x + dx, RING)
        return ((zz * RING + xx) * 2 + lax.rem(c + dc, 2), lax.rem(y + dy, RING))

    up_z, down_z = device(dz=1), device(dz=3)
    up_x, down_x = device(dx=1), device(dx=3)
    up_y, down_y = device(dy=1), device(dy=3)
    sibling = device(dc=1)

    def tell(sem, *where):
        for one in where:
            pl.semaphore_signal(sem, inc=1, device_id=one, device_id_type=MESH)

    barrier = pltpu.get_barrier_semaphore()
    tell(barrier, up_z, down_z, up_x, down_x, sibling, up_y, down_y)

    moves = []
    for p in range(2):
        moves += [
            (trans.at[p], hb.at[p, 0:512]), (amps.at[p], hb.at[p, 512:640]),
            (resp.at[p], hb.at[p, 640:768]),
        ]
    moves += [
        (couple, cg.at[0]), (readers, rg.at[0]), (integrals, xall.at[0]), (domains, dom),
        (ints, ex), (energies, en),
    ]
    copies = [
        pltpu.make_async_copy(src, dst, local_sem.at[i]) for i, (src, dst) in enumerate(moves)
    ]
    for copy in copies:
        copy.start()
    pl.semaphore_wait(barrier, 7)

    sends = []

    def send(src, dst, recv, where):
        copy = pltpu.make_async_remote_copy(
            src_ref=src, dst_ref=dst, send_sem=send_sem.at[len(sends)],
            recv_sem=recv_sem.at[recv], device_id=where, device_id_type=MESH,
        )
        sends.append(copy)
        copy.start()

    def arrive(ref, recv):
        pltpu.make_async_remote_copy(
            src_ref=ref, dst_ref=ref, send_sem=send_sem.at[0],
            recv_sem=recv_sem.at[recv], device_id=sibling, device_id_type=MESH,
        ).wait_recv()

    def send_pair(s, to, where):
        send(hb.at[s], hb.at[to], HB + to, where)

    def arrive_pair(*slots):
        for s in slots:
            arrive(hb.at[s], HB + s)

    PARTS = ((slice(0, 384), HB), (slice(384, 768), HC))

    def send_part(s, part, to, where):
        rows, sem = PARTS[part]
        send(hb.at[s, rows], hb.at[to, rows], sem + to, where)

    def arrive_part(s, part):
        rows, sem = PARTS[part]
        arrive(hb.at[s, rows], sem + s)

    def send_g(src, to, where):
        send(src, qg.at[to], QG + to, where)

    def arrive_g(*slots):
        for s in slots:
            arrive(qg.at[s], QG + s)

    def send_x(d, half, to, where):
        rows = slice(half * 4, half * 4 + 4)
        send(xall.at[d, rows], xall.at[to, rows], XA + to * 2 + half, where)

    def arrive_x(d, half):
        arrive(xall.at[d, half * 4:half * 4 + 4], XA + d * 2 + half)

    def send_own(p, to, where):
        send(trans.at[p], hb.at[to, 0:512], HB + to, where)
        send(amps.at[p], hb.at[to, 512:640], HB + to, where)
        send(resp.at[p], hb.at[to, 640:768], HB + to, where)

    for src, dst, base_sem in ((couple, cg, CG), (readers, rg, RG)):
        send(src, dst.at[3], base_sem + 3, up_x)
        send(src, dst.at[1], base_sem + 1, down_x)
    send_own(0, 4, up_z)
    send_own(1, 5, down_z)
    send_g(trans.at[0], 2, up_x)
    send_g(trans.at[1], 3, down_x)
    send_own(0, 2, sibling)
    send_own(1, 3, sibling)
    send_own(1, 8, up_z)
    send_own(0, 9, down_z)
    send_g(trans.at[1], 4, up_x)
    send_g(trans.at[0], 5, down_x)
    for half, to, where in ((0, 3, up_y), (1, 1, down_y), (1, 3, up_y), (0, 1, down_y)):
        rows = slice(half * 4, half * 4 + 4)
        send(integrals.at[rows], xall.at[to, rows], XA + to * 2 + half, where)
    for copy in copies:
        copy.wait()

    def domain_of(index):
        return [dom[a, index] for a in range(4)]

    zero = jnp.zeros((128, 128), BF16)

    def pair_of_g(k):
        return G_PLACE[k]

    def build_at(k):
        dx, pair = pair_of_g(k)
        own = domain_of((((z * RING + lax.rem(x + dx, RING)) * 2 + c) * RING + y) * 2 + pair)
        source = hb if k < 2 else qg
        turned = [jnp.transpose(source[k, a * 128:(a + 1) * 128, :]) for a in range(4)]
        for block in range(8):
            value = zero
            for a in range(4):
                value = lax.select(own[a] == block, turned[a], value)
            at[block, k * 128:(k + 1) * 128, :] = value

    def place(s):
        group, inner = s // 4, lax.rem(s, 4)
        flip, i = inner // 2, lax.rem(inner, 2)
        near = jnp.where(i == 0, 3, 1)
        dz = jnp.where(group == 0, 0, jnp.where(group == 3, 2, near))
        pair = jnp.where(group == 2, 1 - i, i)
        return lax.rem(z + dz, RING), lax.rem(c + flip, 2), pair

    def index_of(s):
        zz, cc, pair = place(s)
        return (((zz * RING + x) * 2 + cc) * RING + y) * 2 + pair

    def tile(i, low, size=HALF):
        pair = (2 * i, 2 * i + 1)
        inters = []
        for s in pair:
            theirs = domain_of(index_of(s))
            left = jnp.concatenate([at[theirs[b], low:low + size, :] for b in range(4)], axis=1)
            inters.append(dot(left, hb[s, 0:512, :]).astype(BF16))
        for s, inter in zip(pair, inters):
            columns = pl.ds(pl.multiple_of(s * 128, 128), 128)
            both = jnp.concatenate([hb[s, 512:640, :], hb[s, 640:768, :]], axis=1)
            half = dot(inter, both)
            for j in range(size // 128):
                k = low // 128 + j
                rows = slice(j * 128, (j + 1) * 128)
                weight = coef[k, pl.ds(s, 1), :]
                sall[k, :, columns] = inter[rows]
                hall[k, 0:128, columns] = (half[rows, 0:128] * weight).astype(BF16)
                hall[k, 128:256, columns] = (half[rows, 128:256] * weight).astype(BF16)

    def coefficients(ks):
        slots = lax.broadcasted_iota(jnp.int32, (16, 48), 0)
        zz, cc, pair = place(slots)
        position = ((zz * RING + x) * 2 + cc) * 2 + pair
        for k in ks:
            dx, p = pair_of_g(k)
            row = rg[dx, p:p + 1, :]
            weight = cg[dx, p:p + 1, :]
            picked = jnp.where(position == row, weight, 0.0)
            coef[k] = jnp.broadcast_to(jnp.sum(picked, axis=1, keepdims=True), (16, 128))

    build_at(0)
    build_at(1)
    for p in range(2):
        across = jnp.broadcast_to(en[p:p + 1, :], (128, 128))
        denom = across + jnp.transpose(across)
        amp = hb[p, 512:640, :].astype(F32)
        res = hb[p, 640:768, :].astype(F32)
        scale[p] = 0.5 / denom
        base[p, 0] = amp - 0.5 * (ex[p].astype(F32) + denom * amp) / denom
        base[p, 1] = res - 0.5 * (amp + denom * res) / denom
    for src, base_sem in ((cg, CG), (rg, RG)):
        arrive(src.at[3], base_sem + 3)
        send(src.at[3], src.at[2], base_sem + 2, up_x)
        arrive(src.at[1], base_sem + 1)
    tell(known.at[0], up_x, down_x)
    coefficients((0, 1, 2, 3, 4, 5))
    arrive_g(2)
    send_g(qg.at[2], 6, up_x)
    arrive_g(3)
    send_g(qg.at[3], 7, down_x)
    build_at(2)
    build_at(3)
    arrive_pair(2, 3)
    each(0, 2, lambda i: tile(i, 0))
    arrive_x(3, 0)
    send_x(3, 0, 2, up_y)
    arrive_x(1, 1)
    send_x(1, 1, 2, down_y)
    arrive_pair(4)
    send_part(4, 0, 12, up_z)
    send_part(4, 1, 12, up_z)
    send_pair(4, 6, sibling)
    arrive_pair(5)
    send_part(5, 0, 13, down_z)
    send_part(5, 1, 13, down_z)
    send_pair(5, 7, sibling)
    for src, base_sem in ((cg, CG), (rg, RG)):
        arrive(src.at[2], base_sem + 2)
    coefficients((6, 7))
    arrive_g(4, 5)
    build_at(4)
    build_at(5)
    arrive_pair(6, 7)
    each(2, 4, lambda i: tile(i, 0))
    each(0, 4, lambda i: tile(i, HALF, HALF // 2))
    pl.semaphore_wait(known.at[0], 2)
    tell(known.at[1], sibling)
    arrive_g(6, 7)
    build_at(6)
    build_at(7)
    arrive_pair(8)
    send_pair(8, 10, sibling)
    arrive_pair(9)
    send_pair(9, 11, sibling)
    each(0, 4, lambda i: tile(i, HALF + HALF // 2, HALF // 2))
    def hand_on(part):
        for s in (12, 13):
            arrive_part(s, part)
            send_part(s, part, s + 2, sibling)

    def whole(i):
        tile(i, 0)
        tile(i, HALF)

    each(4, 5, whole)
    hand_on(0)
    arrive_pair(10, 11)
    each(5, 6, whole)
    hand_on(1)
    pl.semaphore_wait(known.at[1], 1)
    tell(known.at[2], up_y, down_y)
    each(6, 7, whole)
    for part in range(2):
        for s in (14, 15):
            arrive_part(s, part)
    each(7, 8, whole)

    def coupled(k):
        return dot_nt(hall[k], sall[k])

    for ks in ((6,), (5, 2), (7,), (3, 4)):
        values = [coupled(k) for k in ks]
        for k, value in zip(ks, values):
            dx, p = G_PLACE[k]
            i = dx * 2 - 2 + p
            rs_send[i] = value.astype(BF16)
            send(rs_send.at[i], rs_recv.at[i], RS + i, device(dx=dx))
    pl.semaphore_wait(known.at[2], 2)
    tell(known.at[3], up_y, down_y)
    for d, half in ((3, 1), (1, 0), (2, 0), (2, 1)):
        arrive_x(d, half)

    def columns_of(j):
        p, r = j // 4, lax.rem(j, 4)
        near = jnp.where(r == 1, 4 + 4 * p, 9 - 4 * p)
        s = jnp.where(r == 0, p, jnp.where(r == 3, 12 + p, near))
        theirs = domain_of(index_of(s))
        wide_rows = [
            jnp.concatenate([xall[d, theirs[b]] for d in range(RING)], axis=1) for b in range(4)
        ]
        rows = pl.ds(pl.multiple_of(j * 128, 128), 128)
        yall[rows, :] = dot_tn(hb[s, 0:512, :], jnp.concatenate(wide_rows, axis=0)).astype(BF16)
        for i in range(2):
            value = zero
            for b in range(4):
                value = lax.select(
                    theirs[b] == 2 * z + i, hb[s, b * 128:(b + 1) * 128, :], value
                )
            fsel[j, i * 128:(i + 1) * 128, :] = value

    each(0, 4, columns_of)
    def send_w(s, to, where):
        send(wb.at[s], wb.at[to], WB + to, where)

    for p in range(2):
        total = coupled(p)
        for i in (p, 4 + p, 2 + p):
            arrive(rs_recv.at[i], RS + i)
            total = total + rs_recv[i].astype(F32)
        new_t = base[p, 0] - total[0:128] * scale[p]
        new_z = base[p, 1] - total[128:256] * scale[p]
        out[p * 128:(p + 1) * 128] = new_t
        out[256 + p * 128:384 + p * 128] = new_z
        product = dot_nt(new_t.astype(BF16), new_z.astype(BF16))
        wb[p * 4] = (0.5 * (product + jnp.transpose(product))).astype(BF16)
        send_w(p * 4, p * 4 + 3, device(dz=2))
        send_w(p * 4, p * 4 + 1, up_z)
        send_w(p * 4, p * 4 + 2, down_z)
    pl.semaphore_wait(known.at[3], 2)

    def left_of(*js):
        for j in js:
            lall[:, j * 128:(j + 1) * 128] = dot(fsel[j], wb[j]).astype(BF16)

    each(4, 8, columns_of)
    left_of(0, 4)
    for j in (1, 2, 3):
        arrive(wb.at[j], WB + j)
    left_of(1, 2, 3)
    early = dot(lall[:, 0:512], yall[0:512, :])
    for j in (5, 6, 7):
        arrive(wb.at[j], WB + j)
    left_of(5, 6, 7)

    def piece(i):
        dy, dx, dc = i // 8, (i // 2) % 4, i % 2
        return pltpu.make_async_remote_copy(
            src_ref=obuf.at[dy, lax.rem(x + dx, RING) * 2 + lax.rem(c + dc, 2)],
            dst_ref=rbuf.at[i], send_sem=send_sem.at[PIECE_SEND + i],
            recv_sem=recv_sem.at[PC + i], device_id=device(dx=dx, dc=dc, dy=dy),
            device_id_type=MESH,
        )

    pieces = [None] + [piece(i) for i in range(1, PIECES)]
    for dys in ((2, 3), (0, 1)):
        columns = slice(dys[0] * 128, dys[0] * 128 + 256)
        partial = early[:, columns] + dot(lall[:, 512:1024], yall[512:1024, columns])
        for d in dys:
            for i in range(8):
                block = partial[i * 32:(i + 1) * 32, (d - dys[0]) * 128:(d - dys[0] + 1) * 128]
                obuf[d, i] = block.astype(BF16)
        for d in dys:
            for i in (4, 5, 2, 3, 6, 7, 1, 0):
                if d * 8 + i:
                    pieces[d * 8 + i].start()
    for copy in sends:
        copy.wait_send()
    total = obuf[0, x * 2 + c].astype(F32)
    for i in range(1, PIECES):
        pieces[i].wait_recv()
        total = total + rbuf[i].astype(F32)
    out[512:544] = total
    for i in range(1, PIECES):
        pieces[i].wait_send()


def per_device(amps, resp, trans, ints, energies, couple, readers, domains, integrals):
    anywhere = pl.BlockSpec(memory_space=pltpu.HBM)
    vmem = pl.BlockSpec(memory_space=pltpu.VMEM)
    dma = pltpu.SemaphoreType.DMA
    out = pl.pallas_call(
        kernel,
        out_shape=jax.ShapeDtypeStruct((544, 128), F32),
        in_specs=[anywhere] * 9,
        out_specs=vmem,
        scratch_shapes=[
            pltpu.VMEM((16, 768, 128), BF16),
            pltpu.VMEM((8, 512, 128), BF16),
            pltpu.VMEM((8, 1024, 128), BF16),
            pltpu.VMEM((8, 128, 2048), BF16),
            pltpu.VMEM((8, 256, 2048), BF16),
            pltpu.VMEM((4, 8, 128, 128), BF16),
            pltpu.VMEM((1024, 512), BF16),
            pltpu.VMEM((8, 256, 128), BF16),
            pltpu.VMEM((256, 1024), BF16),
            pltpu.VMEM((8, 128, 128), BF16),
            pltpu.VMEM((8, 16, 128), F32),
            pltpu.VMEM((4, 2, 48), F32),
            pltpu.VMEM((4, 2, 48), jnp.int32),
            pltpu.SMEM((4, 256), jnp.int32),
            pltpu.VMEM((2, 128, 128), BF16),
            pltpu.VMEM((2, 128), F32),
            pltpu.VMEM((2, 2, 128, 128), F32),
            pltpu.VMEM((2, 128, 128), F32),
            pltpu.VMEM((6, 256, 128), BF16),
            pltpu.VMEM((6, 256, 128), BF16),
            pltpu.VMEM((4, 8, 32, 128), BF16),
            pltpu.VMEM((PIECES, 32, 128), BF16),
            dma((16,)), dma((N_SEND,)), dma((N_RECV,)), pltpu.SemaphoreType.REGULAR((4,)),
        ],
        compiler_params=pltpu.CompilerParams(
            collective_id=0, has_side_effects=True, vmem_limit_bytes=32 * 1024 * 1024
        ),
    )(
        *(
            pltpu.with_memory_space_constraint(value, pltpu.HBM)
            for value in (
                amps, resp, trans, ints, energies, couple, readers, domains.T,
                integrals.reshape(8, 128, 128),
            )
        )
    )
    return (
        out[0:256].reshape(2, 128, 128), out[256:512].reshape(2, 128, 128), out[512:544],
    )


def solution(mesh):
    pairs3 = P(("wide", "narrow"), None, None)
    pairs2 = P(("wide", "narrow"), None)
    return jax.shard_map(
        per_device,
        mesh=mesh,
        in_specs=(
            pairs3, pairs3, pairs3, pairs3, pairs2, pairs2, pairs2, P(), P(None, "narrow"),
        ),
        out_specs=(pairs3, pairs3, P("wide", "narrow")),
        check_vma=False,
    )
```
